32 devices in a mesh: dom: 16 (over z, x, core), band: 2 (over y).
Axes of the slice: x: 2, y: 2, z: 4, core: 2. Of those that a mesh axis runs over, the one named last changes fastest.
Arguments:
- wavefun: float32 [13824, 512], P('dom', 'band')
- cell_ops: float32 [64, 343, 343], P('dom'), as said below
- cell_map: int32 [64, 343], P('dom'), may hold values from 0 to 1007, as said below
- face_list: int32 [2304], P('dom'), may hold values from 0 to 863, as said below
Outputs:
- ortho_bands: float32 [13824, 512], P('dom', 'band')
The draws below stay inside these ranges and needn't reach their ends.
Inputs may be any that keep to these rules, and one draw needn't show every extreme that they name: `cell_map`: each row lists the 343 distinct local numbers of a cell's nodes; a number below 864 is a node of the cell's own domain, 864 + j stands for the j-th lower face node of the next domain (periodic over domains); every node of a domain belongs to some cell of that domain. `face_list`: the 144 entries of each domain are distinct node numbers of that domain. `cell_ops`: each cell's matrix is symmetric.
All inputs are finite; a program needn't handle non-finite values.
Results may differ from the reference program's by a relative error of at most 0.0001.
Values sent between devices are 32-bit elements; how exact they have to be, the bound alone decides.
A program may use at most 64 MiB of HBM per device.

```python
import math
import jax
import jax.numpy as jnp
from jax import lax

P_SIZE = 6
LX = 1
NB = 512
DEGREE = 2
NODE_CELL = 343
FACE = 144
OWN = 864
CELLS = 4
DOMAINS = 16
NODES = 13824
ALL_CELLS = 64


def geometry(key):
    geo_key = jax.random.fold_in(key, 11)
    side = 2 * P_SIZE
    layers = P_SIZE * LX
    per_side = P_SIZE + 1
    cell_index = jnp.arange(CELLS, dtype=jnp.int32)[:, None]
    node_index = jnp.arange(NODE_CELL, dtype=jnp.int32)[None, :]
    cell_x = cell_index // 4
    cell_y = cell_index // 2 % 2
    cell_z = cell_index % 2
    along_a = node_index // (per_side * per_side)
    along_b = node_index // per_side % per_side
    along_e = node_index % per_side
    pos_x = cell_x * P_SIZE + along_a
    pos_y = (cell_y * P_SIZE + along_b) % side
    pos_z = (cell_z * P_SIZE + along_e) % side
    geo_index = jnp.clip((pos_x * side + pos_y) * side + pos_z, 0, OWN - 1).reshape(-1)
    face_index = (pos_y * side + pos_z).reshape(-1)
    inside = (pos_x < layers).reshape(-1)
    domain_keys = jax.random.split(geo_key, DOMAINS)
    labels = jax.vmap(lambda one_key: jax.random.permutation(one_key, OWN).astype(jnp.int32))(domain_keys)
    mapped = jnp.where(inside[None, :], labels[:, geo_index], OWN + face_index[None, :])
    cell_table = mapped.reshape(ALL_CELLS, NODE_CELL).astype(jnp.int32)
    face_table = labels[:, :FACE].reshape(-1).astype(jnp.int32)
    return (cell_table, face_table)


def draw_cell_map(key, part):
    return geometry(key)[0]


def draw_face_list(key, part):
    return geometry(key)[1]


def draw_cell_ops(key, part):
    ops_key = jax.random.fold_in(key, 5)
    noise_key, diag_key = jax.random.split(ops_key)
    noise = jax.random.normal(noise_key, (ALL_CELLS, NODE_CELL, NODE_CELL), jnp.float32)
    symmetric = (noise + jnp.swapaxes(noise, 1, 2)) / math.sqrt(2.0) * (0.055 / math.sqrt(NODE_CELL))
    diagonal = jax.random.uniform(diag_key, (ALL_CELLS, NODE_CELL), jnp.float32, 0.05, 0.2)
    identity = jnp.eye(NODE_CELL, dtype=jnp.float32)
    return symmetric + diagonal[:, :, None] * identity[None, :, :]


def draw_wavefun(key, part):
    wave_key = jax.random.fold_in(key, 3)
    keys = jax.random.split(wave_key, 5)
    base = jax.random.normal(keys[0], (NODES, NB), jnp.float32)
    common_weight = 0.5
    column_scale = jnp.exp(jax.random.uniform(keys[1], (NB,), jnp.float32, math.log(0.5), math.log(5.0)))
    row_rand = jnp.exp(jax.random.uniform(keys[2], (NODES,), jnp.float32, math.log(0.3), math.log(3.0)))
    domain_pos = (jnp.arange(NODES, dtype=jnp.int32) // OWN).astype(jnp.float32)
    row_scale = row_rand * (1.0 + 2.0 * domain_pos / (DOMAINS - 1)) / 2.0
    common_left = jax.random.normal(keys[3], (NODES, 48), jnp.float32)
    common_right = jax.random.normal(keys[4], (48, NB), jnp.float32) / math.sqrt(48.0)
    common = jnp.dot(common_left, common_right)
    return row_scale[:, None] * (base * column_scale[None, :] + common_weight * common)


def setup_inputs(seed: int = 0) -> dict:
    key_of = jax.random.split(jax.random.key(seed), 5)
    return {
        "wavefun": draw_wavefun(jax.random.fold_in(key_of[4], 71), 0),
        "cell_ops": draw_cell_ops(jax.random.fold_in(key_of[4], 71), 0),
        "cell_map": draw_cell_map(jax.random.fold_in(key_of[4], 71), 0),
        "face_list": draw_face_list(jax.random.fold_in(key_of[4], 71), 0),
    }


cheb_centre = 1.0
cheb_half = 1.6

def reference(wavefun, cell_ops, cell_map, face_list):
    domain_of = jnp.arange(ALL_CELLS, dtype=jnp.int32) // CELLS
    next_domain = (domain_of + 1) % DOMAINS
    face_slot = jnp.clip(cell_map - OWN, 0, FACE - 1).astype(jnp.int32)
    neighbour_node = next_domain[:, None] * OWN + face_list[next_domain[:, None] * FACE + face_slot]
    global_node = jnp.where(cell_map < OWN, domain_of[:, None] * OWN + cell_map, neighbour_node).astype(jnp.int32)
    flat_nodes = global_node.reshape(-1)

    def operate(vector):

        def one_domain(domain_index):
            nodes = lax.dynamic_slice_in_dim(global_node, domain_index * CELLS, CELLS, 0)
            matrices = lax.dynamic_slice_in_dim(cell_ops, domain_index * CELLS, CELLS, 0)
            gathered = vector[nodes]
            return jnp.einsum('cij,cjb->cib', matrices, gathered, precision=lax.Precision.HIGHEST)
        products = lax.map(one_domain, jnp.arange(DOMAINS, dtype=jnp.int32))
        return jnp.zeros_like(vector).at[flat_nodes].add(products.reshape(-1, NB))
    earlier = wavefun
    latest = (operate(wavefun) - cheb_centre * wavefun) / cheb_half
    for counter in range(1, DEGREE):
        following = 2.0 * (operate(latest) - cheb_centre * latest) / cheb_half - earlier
        earlier = latest
        latest = following
    filtered = latest
    margin = jnp.einsum('nb,nc->bc', filtered, filtered, precision=lax.Precision.HIGHEST)
    norm_value = jnp.sqrt(jnp.sum(margin * margin) + 1e-06)
    scaled = margin / norm_value
    identity = jnp.eye(NB, dtype=jnp.float32)
    mixing = (3.0 * identity - scaled) / 2.0
    return jnp.dot(filtered, mixing, precision=lax.Precision.HIGHEST)
```

```python
import functools
import types

import jax
import jax.numpy as jnp
from jax import lax
from jax.experimental import pallas as pl
from jax.experimental.pallas import tpu as pltpu
from jax.sharding import PartitionSpec as P

DEGREE = 2


cheb_centre = 1.0
cheb_half = 1.6

f32 = jnp.float32
bf16 = jnp.bfloat16
MESH = pl.DeviceIdType.MESH


def round_up(value, step):
    return (value + step - 1) // step * step


def halves(value):
    high = value.astype(bf16)
    low = (value - high.astype(f32)).astype(bf16)
    return high, low


def dot(left, right):
    return jnp.dot(left, right, preferred_element_type=f32)


def dot_tn(left, right):
    return lax.dot_general(left, right, (((0,), (0,)), ((), ())), preferred_element_type=f32)


def dot_nt(left, right):
    return lax.dot_general(left, right, (((1,), (1,)), ((), ())), preferred_element_type=f32)


class Sizes:
    def __init__(self, n_dom, n_band, own, width, cells, nodes, face):
        self.n_dom, self.n_band = n_dom, n_band
        self.own, self.width = own, width
        self.cells, self.nodes, self.face = cells, nodes, face
        self.own_pad = round_up(own, 128)
        self.face_pad = round_up(face, 128)
        self.rows = round_up(nodes, 16)
        self.lanes = round_up(nodes, 128)
        self.blocks = 2 if width % 256 == 0 else 1
        self.block = width // self.blocks
        self.depth = round_up(own + face, 128)
        self.base = own // 128 * 128
        self.half_pad = round_up(own // 2, 128)
        self.chips = n_dom // 2
        self.chunk = width // n_dom
        self.packet = self.chunk + 8
        self.gram = (
            n_band == 2
            and n_dom % 2 == 0
            and n_dom > 2
            and width % (8 * n_dom) == 0
            and width % 128 == 0
            and own % 32 == 0
        )


def start_all(copies):
    for copy in copies:
        copy.start()


def wait_all(copies):
    for copy in copies:
        copy.wait()


def filter_steps(s, ready, done, wave_ref, ops_ref, map_ref, face_ref, result_ref, w):
    me = lax.axis_index("dom")
    right = lax.rem(me + 1, s.n_dom)
    left = lax.rem(me + s.n_dom - 1, s.n_dom)
    C, R, L, W = s.cells, s.rows, s.lanes, s.block
    known = s.own + s.face

    def split_store(ref, first, value):
        high, low = halves(value)
        ref[pl.ds(first, value.shape[0]), pl.ds(0, W)] = high
        ref[pl.ds(first, value.shape[0]), pl.ds(W, W)] = low

    def merged(wide):
        return wide[:, :W] + wide[:, W:]

    ops_copy = pltpu.make_async_copy(ops_ref, w.ops, w.ops_sem)
    ops_copy.start()

    w.index[...] = jnp.full(w.index.shape, -1.0, f32)
    w.index[pl.ds(0, C), pl.ds(0, s.nodes)] = map_ref[...].astype(f32)
    w.index[pl.ds(C, 1), pl.ds(0, s.face)] = face_ref[...].astype(f32)
    columns = jnp.transpose(w.index[...])

    def one_hot(match):
        return jnp.where(match, 1.0, 0.0).astype(bf16)

    def iota(shape, axis):
        return lax.broadcasted_iota(jnp.int32, shape, axis).astype(f32)

    faces = columns[: s.face, C : C + 1]
    w.face_rows[...] = one_hot(faces == iota((s.face, s.own_pad), 1))
    for q in range(s.blocks):
        w.vec[q, pl.ds(s.own, s.depth - s.own), :] = jnp.zeros((s.depth - s.own, 2 * W), bf16)
        split_store(w.vec.at[q], 0, wave_ref[:, pl.ds(q * W, W)])
        w.face_send[q] = merged(dot(w.face_rows[...], w.vec[q, pl.ds(0, s.own_pad), :]))

    def remote(send, recv, send_sem, recv_sem, target):
        return pltpu.make_async_remote_copy(
            src_ref=send, dst_ref=recv, send_sem=send_sem, recv_sem=recv_sem,
            device_id={"dom": target}, device_id_type=MESH)

    def face_copy(q):
        return remote(w.face_send.at[q], w.face_recv.at[q], w.face_ssem.at[q], w.face_rsem.at[q], left)

    def back_copy(step, q):
        return remote(w.back_send.at[step, q], w.back_recv.at[step, q],
                      w.back_ssem.at[step, q], w.back_rsem.at[step, q], right)

    def edge_copy(step, q):
        return remote(w.edge_send.at[step, q], w.edge_recv.at[step, q],
                      w.edge_ssem.at[step, q], w.edge_rsem.at[step, q], left)

    def setup_take():
        for c in range(C):
            w.take[pl.ds(c * R, R), :] = one_hot(columns[:R, c : c + 1] == iota((R, s.depth), 1))

    def setup_ops():
        w.op_pad[...] = jnp.zeros(w.op_pad.shape, f32)
        ops_copy.wait()
        for c in range(C):
            w.op_pad[c, pl.ds(0, s.nodes), pl.ds(0, s.nodes)] = w.ops[:, c, :]
            high, low = halves(w.op_pad[c])
            w.op_high[c] = high
            w.op_low[c] = low

    def setup_put():
        for c in range(C):
            row = w.index[c : c + 1, pl.ds(0, L)]
            w.put[pl.ds(0, known), pl.ds(c * L, L)] = one_hot(row == iota((known, L), 0))
            w.put[pl.ds(known, s.face), pl.ds(c * L, L)] = one_hot(row == faces)
            if L > R:
                for q in range(s.blocks):
                    w.prod[q, pl.ds(c * L + R, L - R), :] = jnp.zeros((L - R, 2 * W), bf16)
                w.cell[c, pl.ds(R, L - R), :] = jnp.zeros((L - R, 2 * W), bf16)
        w.put_back[...] = one_hot(w.index[C : C + 1, pl.ds(0, s.face_pad)] == iota((s.own, s.face_pad), 0))
        for q in range(s.blocks):
            w.far[q] = jnp.zeros(w.far.shape[1:], bf16)
            if s.face_pad > s.face:
                w.back[q, pl.ds(s.face, s.face_pad - s.face), :] = jnp.zeros((s.face_pad - s.face, 2 * W), bf16)

    def gather(q):
        w.part[q] = dot(w.take[:, pl.ds(0, s.own_pad)], w.vec[q, pl.ds(0, s.own_pad), :])

    def middle(step, q):
        last = step == DEGREE - 1
        if step == 0:
            face_copy(q).wait()
            split_store(w.far.at[q], s.own - s.base, w.face_recv[q])
        for c in range(C):
            rows = pl.ds(c * R, R)
            if step == 0:
                cell = w.part[q, rows, :] + dot(w.take[rows, pl.ds(s.base, s.depth - s.base)], w.far[q])
            else:
                cell = dot(w.take[rows, :], w.vec[q])
            w.cell[c, pl.ds(0, R), :] = cell.astype(bf16)
        for c in range(C):
            wide = dot(w.op_high[c], w.cell[c])
            value = wide[:, :W] + wide[:, W:] + dot(w.op_low[c], w.cell[c, :, pl.ds(0, W)])
            split_store(w.prod.at[q], c * L, value)
        count = s.face if last else 2 * s.face
        tail = merged(dot(w.put[pl.ds(s.own, count), :], w.prod[q]))
        w.back_send[step, q] = tail[: s.face]
        back_copy(step, q).start()
        if not last:
            w.edge_send[step, q] = tail[s.face :]
            edge_copy(step, q).start()

    def scatter(q):
        w.applied[q] = merged(dot(w.put[pl.ds(0, s.own), :], w.prod[q]))

    def advance(step, applied, current, earlier):
        if step == 0:
            return (applied - cheb_centre * current) / cheb_half
        return 2.0 * (applied - cheb_centre * current) / cheb_half - earlier

    def finish(step, q):
        back_copy(step, q).wait()
        split_store(w.back.at[q], 0, w.back_recv[step, q])
        applied = w.applied[q] + merged(dot(w.put_back[...], w.back[q]))
        columns = pl.ds(q * W, W)

        def stage(k):
            return wave_ref[:, columns] if k == 0 else w.stages[k - 1, :, columns]

        following = advance(step, applied, stage(step), stage(step - 1) if step else None)
        if step == DEGREE - 1:
            result_ref[:, columns] = following
            done(q)
            return
        w.stages[step, :, columns] = following
        split_store(w.vec.at[q], 0, following)
        edge_copy(step, q).wait()

        def edge(k):
            return w.face_recv[q] if k == 0 else w.edges[k - 1, q]

        outer = advance(step, w.back_send[step, q] + w.edge_recv[step, q], edge(step), edge(step - 1) if step else None)
        w.edges[step, q] = outer
        split_store(w.vec.at[q], s.own, outer)

    blocks = range(s.blocks)
    setup_take()
    setup_ops()
    setup_put()
    ready()
    for q in blocks:
        face_copy(q).start()
    for q in blocks:
        gather(q)
    for q in blocks:
        middle(0, q)
    for q in blocks:
        scatter(q)
    for step in range(1, DEGREE):
        for q in blocks:
            finish(step - 1, q)
            middle(step, q)
        if step < DEGREE - 1:
            for q in blocks:
                scatter(q)
    for q in blocks:
        scatter(q)
        finish(DEGREE - 1, q)


def band_copy(s, band_ref, w, turn, first, q):
    half = s.own // 2
    rows = pl.ds(pl.multiple_of(first * half, 8), half)
    columns = pl.ds(q * s.block, s.block)
    return pltpu.make_async_remote_copy(
        src_ref=band_ref.at[rows, columns], dst_ref=w.far_band.at[rows, columns],
        send_sem=w.band_ssem.at[turn, q], recv_sem=w.band_rsem.at[turn, q],
        device_id={"band": 1 - lax.axis_index("band")}, device_id_type=MESH)


def gram_steps(s, band_ref, out_ref, w):
    me = lax.axis_index("dom")
    band = lax.axis_index("band")
    other = 1 - band
    chip, core = me // 2, lax.rem(me, 2)
    partner = chip * 2 + (1 - core)
    W, half, n, chunk = s.width, s.own // 2, s.chips, s.chunk

    def core_copy(m):
        return pltpu.make_async_remote_copy(
            src_ref=w.sums.at[m, 1 - core], dst_ref=w.core_recv.at[m],
            send_sem=w.core_ssem.at[m], recv_sem=w.core_rsem.at[m],
            device_id={"dom": partner}, device_id_type=MESH)

    def scatter_copies(m):
        copies = []
        for j in range(1, n):
            target = lax.rem(chip + j, n)
            copies.append(pltpu.make_async_remote_copy(
                src_ref=w.pair.at[m, target], dst_ref=w.scat_recv.at[m, j - 1],
                send_sem=w.scat_ssem.at[m, j - 1], recv_sem=w.scat_rsem.at[m, j - 1],
                device_id={"dom": target * 2 + core}, device_id_type=MESH))
        return copies

    def gather_copies(m):
        copies = []
        for j in range(1, n):
            target = lax.rem(chip + j, n)
            copies.append(pltpu.make_async_remote_copy(
                src_ref=w.full.at[m, core, chip], dst_ref=w.full.at[m, core, chip],
                send_sem=w.gath_ssem.at[m, j - 1], recv_sem=w.gath_rsem.at[m, j - 1],
                device_id={"dom": target * 2 + core}, device_id_type=MESH))
        return copies

    def swap_copy(m):
        return pltpu.make_async_remote_copy(
            src_ref=w.full.at[m, core], dst_ref=w.full.at[m, core],
            send_sem=w.swap_ssem.at[m], recv_sem=w.swap_rsem.at[m],
            device_id={"dom": partner}, device_id_type=MESH)

    def cross_copy():
        return pltpu.make_async_remote_copy(
            src_ref=w.cross_send, dst_ref=w.cross_recv,
            send_sem=w.cross_ssem, recv_sem=w.cross_rsem,
            device_id={"band": other}, device_id_type=MESH)

    def put_sums(m, value):
        w.sums[m] = value.reshape(2, W // 2, W)

    def pair_up(m):
        core_copy(m).wait()
        total = w.sums[m, core] + w.core_recv[m]
        w.pair[m] = total.reshape(n, chunk, W)

    def own_total(m):
        wait_all(scatter_copies(m))
        total = w.pair[m, chip]
        for j in range(n - 1):
            total = total + w.scat_recv[m, j]
        return total

    high, low = halves(band_ref[...])
    def fill(ref, value):
        count, size = value.shape[0], ref.shape[0]
        ref[pl.ds(0, count), :] = value
        if size > count:
            ref[pl.ds(count, size - count), :] = jnp.zeros((size - count, W), bf16)

    fill(w.near_high, high)
    fill(w.near_low, low)
    turned_high, turned_low = halves(jnp.transpose(w.bands[...]))
    put_sums(0, dot(turned_high, w.near_high[...])
             + dot(turned_high, w.near_low[...])
             + dot(turned_low, w.near_high[...]))
    core_copy(0).start()
    pair_up(0)
    start_all(scatter_copies(0))
    same = own_total(0)
    w.full[0, core, chip, pl.ds(0, chunk), :] = same
    squares = (same * same).reshape(chunk // 8, 8, W).sum(0)
    w.full[0, core, chip, pl.ds(chunk, 8), :] = squares
    start_all(gather_copies(0))

    for q in range(s.blocks):
        band_copy(s, band_ref, w, 0, other, q).wait_send()
        band_copy(s, band_ref, w, 0, band, q).wait_recv()
    for q in range(s.blocks):
        band_copy(s, band_ref, w, 1, band, q).start()
    rows = pl.ds(pl.multiple_of(band * half, 16), half)
    far_high, far_low = halves(w.far_band[rows, :])
    near_high, near_low = w.near_high[rows, :], w.near_low[rows, :]
    first = band == 0

    def pick(a, b):
        return jnp.where(first, a, b)

    fill(w.left_high, pick(far_high, near_high))
    fill(w.left_low, pick(far_low, near_low))
    fill(w.right_high, pick(near_high, far_high))
    fill(w.right_low, pick(near_low, far_low))
    put_sums(1, dot_tn(w.left_high[...], w.right_high[...])
             + dot_tn(w.left_high[...], w.right_low[...])
             + dot_tn(w.left_low[...], w.right_high[...]))
    core_copy(1).start()
    pair_up(1)
    start_all(scatter_copies(1))

    wait_all(gather_copies(0))
    swap_copy(0).start()
    cross = own_total(1)
    w.cross_send[pl.ds(0, chunk), :] = cross
    w.cross_send[pl.ds(chunk, 8), :] = squares
    cross_copy().start()
    cross_copy().wait()
    cross = pick(cross, w.cross_recv[pl.ds(0, chunk), :]) + pick(w.cross_recv[pl.ds(0, chunk), :], cross)
    w.full[1, core, chip, pl.ds(0, chunk), :] = cross
    w.full[1, core, chip, pl.ds(chunk, 8), :] = (
        2.0 * (cross * cross).reshape(chunk // 8, 8, W).sum(0) + w.cross_recv[pl.ds(chunk, 8), :])
    start_all(gather_copies(1))
    swap_copy(0).wait()
    near_block = w.full[0, :, :, pl.ds(0, chunk), :].reshape(W, W)
    block_high, block_low = halves(near_block)
    w.block_high[0] = block_high
    w.block_low[0] = block_low
    near_high, near_low = w.near_high[pl.ds(0, s.own), :], w.near_low[pl.ds(0, s.own), :]
    near_wide = dot(near_high, w.block_high[0]) + dot(near_high, w.block_low[0])
    w.near_prod[...] = near_wide + dot(near_low, w.block_high[0])
    for q in range(s.blocks):
        band_copy(s, band_ref, w, 1, band, q).wait_send()
        band_copy(s, band_ref, w, 1, other, q).wait_recv()
    high, low = halves(w.far_band[...])
    w.far_high[...] = high
    w.far_low[...] = low
    wait_all(gather_copies(1))
    swap_copy(1).start()
    swap_copy(1).wait()
    total = jnp.sum(w.full[:, :, :, pl.ds(chunk, 8), :])
    norm = jnp.sqrt(jnp.full((1, W), total, f32) + 1e-06)
    far_block = w.full[1, :, :, pl.ds(0, chunk), :].reshape(W, W)
    far_block = pick(far_block, jnp.transpose(far_block))
    block_high, block_low = halves(far_block)
    w.block_high[1] = block_high
    w.block_low[1] = block_low
    wide = dot(w.far_high[...], w.block_high[1]) + dot(w.far_high[...], w.block_low[1])
    wide = wide + dot(w.far_low[...], w.block_high[1]) + w.near_prod[...]
    out_ref[...] = 1.5 * band_ref[...] - wide * (0.5 / norm)


def kernel(s, names, wave_ref, ops_ref, map_ref, face_ref, out_ref, *scratch):
    w = types.SimpleNamespace(**dict(zip(names, scratch)))
    me = lax.axis_index("dom")
    barrier = pltpu.get_barrier_semaphore()
    greeted = [{"dom": lax.rem(me + 1, s.n_dom)}, {"dom": lax.rem(me + s.n_dom - 1, s.n_dom)}]
    if s.gram:
        chip, core = me // 2, lax.rem(me, 2)
        greeted.append({"dom": chip * 2 + (1 - core)})
        greeted.append({"band": 1 - lax.axis_index("band")})
        for j in range(1, s.chips):
            greeted.append({"dom": lax.rem(chip + j, s.chips) * 2 + core})
    for device in greeted:
        pl.semaphore_signal(barrier, inc=1, device_id=device, device_id_type=MESH)

    def ready():
        pl.semaphore_wait(barrier, len(greeted))

    if s.gram:
        if s.own_pad > s.own:
            w.bands[pl.ds(s.own, s.own_pad - s.own), :] = jnp.zeros((s.own_pad - s.own, s.width), f32)
        owned = w.bands.at[pl.ds(0, s.own), :]

        def send(q):
            band_copy(s, owned, w, 0, 1 - lax.axis_index("band"), q).start()

        filter_steps(s, ready, send, wave_ref, ops_ref, map_ref, face_ref, owned, w)
        gram_steps(s, owned, out_ref, w)
    else:
        filter_steps(s, ready, lambda q: None, wave_ref, ops_ref, map_ref, face_ref, out_ref, w)


def scratch_of(s):
    C, R, L, W, n, chunk = s.cells, s.rows, s.lanes, s.width, s.chips, s.chunk
    V, dma = pltpu.VMEM, pltpu.SemaphoreType.DMA
    scratch = dict(
        index=V((128, max(L, s.face_pad)), f32),
        face_rows=V((s.face, s.own_pad), bf16),
        vec=V((s.blocks, s.depth, 2 * s.block), bf16),
        take=V((C * R, s.depth), bf16),
        put=V((s.own + 2 * s.face, C * L), bf16),
        put_back=V((s.own, s.face_pad), bf16),
        ops=V((s.nodes, C, s.nodes), f32),
        ops_sem=dma,
        op_pad=V((C, R, L), f32),
        op_high=V((C, R, L), bf16),
        op_low=V((C, R, L), bf16),
        part=V((s.blocks, C * R, 2 * s.block), f32),
        applied=V((s.blocks, s.own, s.block), f32),
        cell=V((C, L, 2 * s.block), bf16),
        prod=V((s.blocks, C * L, 2 * s.block), bf16),
        far=V((s.blocks, s.depth - s.base, 2 * s.block), bf16),
        back=V((s.blocks, s.face_pad, 2 * s.block), bf16),
        stages=V((DEGREE - 1, s.own, W), f32),
        edges=V((DEGREE - 1, s.blocks, s.face, s.block), f32),
        face_send=V((s.blocks, s.face, s.block), f32),
        face_recv=V((s.blocks, s.face, s.block), f32),
        edge_send=V((DEGREE - 1, s.blocks, s.face, s.block), f32),
        edge_recv=V((DEGREE - 1, s.blocks, s.face, s.block), f32),
        back_send=V((DEGREE, s.blocks, s.face, s.block), f32),
        back_recv=V((DEGREE, s.blocks, s.face, s.block), f32),
        face_ssem=dma((s.blocks,)),
        face_rsem=dma((s.blocks,)),
        edge_ssem=dma((DEGREE - 1, s.blocks)),
        edge_rsem=dma((DEGREE - 1, s.blocks)),
        back_ssem=dma((DEGREE, s.blocks)),
        back_rsem=dma((DEGREE, s.blocks)),
    )
    if s.gram:
        scratch |= dict(
            bands=V((s.own_pad, W), f32),
            far_band=V((s.own, W), f32),
            near_high=V((s.own_pad, W), bf16),
            near_low=V((s.own_pad, W), bf16),
            left_high=V((s.half_pad, W), bf16),
            left_low=V((s.half_pad, W), bf16),
            right_high=V((s.half_pad, W), bf16),
            right_low=V((s.half_pad, W), bf16),
            far_high=V((s.own, W), bf16),
            far_low=V((s.own, W), bf16),
            near_prod=V((s.own, W), f32),
            block_high=V((2, W, W), bf16),
            block_low=V((2, W, W), bf16),
            sums=V((2, 2, W // 2, W), f32),
            core_recv=V((2, W // 2, W), f32),
            pair=V((2, n, chunk, W), f32),
            scat_recv=V((2, n - 1, chunk, W), f32),
            full=V((2, 2, n, s.packet, W), f32),
            cross_send=V((s.packet, W), f32),
            cross_recv=V((s.packet, W), f32),
            cross_ssem=dma,
            cross_rsem=dma,
            band_ssem=dma((2, s.blocks)),
            band_rsem=dma((2, s.blocks)),
            core_ssem=dma((2,)),
            core_rsem=dma((2,)),
            swap_ssem=dma((2,)),
            swap_rsem=dma((2,)),
            scat_ssem=dma((2, n - 1)),
            scat_rsem=dma((2, n - 1)),
            gath_ssem=dma((2, n - 1)),
            gath_rsem=dma((2, n - 1)),
        )
    return scratch


def on_device(wavefun, cell_ops, cell_map, face_list):
    s = Sizes(lax.axis_size("dom"), lax.axis_size("band"), wavefun.shape[0], wavefun.shape[1],
              cell_map.shape[0], cell_map.shape[1], face_list.shape[0])
    scratch = scratch_of(s)
    latest = pl.pallas_call(
        functools.partial(kernel, s, list(scratch)),
        out_shape=jax.ShapeDtypeStruct(wavefun.shape, f32),
        in_specs=[pl.BlockSpec(memory_space=space) for space in (pltpu.VMEM, pl.ANY, pltpu.VMEM, pltpu.VMEM)],
        out_specs=pl.BlockSpec(memory_space=pltpu.VMEM),
        scratch_shapes=list(scratch.values()),
        compiler_params=pltpu.CompilerParams(
            collective_id=0, has_side_effects=True, vmem_limit_bytes=60 * 1024 * 1024),
        name="filtered_bands",
    )(wavefun, jnp.swapaxes(cell_ops, 0, 1), cell_map, face_list.reshape(1, -1))
    if s.gram:
        return latest
    full_bands = lax.all_gather(latest, "band", axis=1, tiled=True)
    partial_value = jnp.einsum("nb,nc->bc", full_bands, full_bands, precision=lax.Precision.HIGHEST)
    margin = lax.psum(partial_value, "dom")
    norm_value = jnp.sqrt(jnp.sum(margin * margin) + 1e-06)
    full_width = margin.shape[0]
    offset = lax.axis_index("band") * s.width
    scaled_cols = lax.dynamic_slice_in_dim(margin, offset, s.width, 1) / norm_value
    identity_cols = lax.dynamic_slice_in_dim(
        jnp.eye(full_width, dtype=jnp.float32), offset, s.width, 1
    )
    mixing = (3.0 * identity_cols - scaled_cols) / 2.0
    return jnp.dot(full_bands, mixing, precision=lax.Precision.HIGHEST)


def solution(mesh):
    return jax.shard_map(
        on_device,
        mesh=mesh,
        in_specs=(P("dom", "band"), P("dom", None, None), P("dom", None), P("dom")),
        out_specs=P("dom", "band"),
        check_vma=False,
    )
```

```python
import functools
import types

import jax
import jax.numpy as jnp
from jax import lax
from jax.experimental import pallas as pl
from jax.experimental.pallas import tpu as pltpu
from jax.sharding import PartitionSpec as P

DEGREE = 2


cheb_centre = 1.0
cheb_half = 1.6

f32 = jnp.float32
bf16 = jnp.bfloat16
MESH = pl.DeviceIdType.MESH


def round_up(value, step):
    return (value + step - 1) // step * step


def halves(value):
    high = value.astype(bf16)
    low = (value - high.astype(f32)).astype(bf16)
    return high, low


def dot(left, right):
    return jnp.dot(left, right, preferred_element_type=f32)


def dot_tn(left, right):
    return lax.dot_general(left, right, (((0,), (0,)), ((), ())), preferred_element_type=f32)


def dot_nt(left, right):
    return lax.dot_general(left, right, (((1,), (1,)), ((), ())), preferred_element_type=f32)


class Sizes:
    def __init__(self, n_dom, n_band, own, width, cells, nodes, face):
        self.n_dom, self.n_band = n_dom, n_band
        self.own, self.width = own, width
        self.cells, self.nodes, self.face = cells, nodes, face
        self.own_pad = round_up(own, 128)
        self.face_pad = round_up(face, 128)
        self.rows = round_up(nodes, 16)
        self.lanes = round_up(nodes, 128)
        self.blocks = 2 if width % 256 == 0 else 1
        self.block = width // self.blocks
        self.depth = round_up(own + face, 128)
        self.base = own // 128 * 128
        self.half_pad = round_up(own // 2, 128)
        self.chips = n_dom // 2
        self.chunk = width // n_dom
        self.gram = (
            n_band == 2
            and n_dom % 2 == 0
            and n_dom > 2
            and width % (8 * n_dom) == 0
            and width % 128 == 0
            and own % 32 == 0
        )


def start_all(copies):
    for copy in copies:
        copy.start()


def wait_all(copies):
    for copy in copies:
        copy.wait()


def filter_steps(s, greet, ready, done, wave_ref, ops_ref, map_ref, face_ref, result_ref, w):
    me = lax.axis_index("dom")
    right = lax.rem(me + 1, s.n_dom)
    left = lax.rem(me + s.n_dom - 1, s.n_dom)
    C, R, L, W = s.cells, s.rows, s.lanes, s.block
    known = s.own + s.face
    blocks = range(s.blocks)

    def span(q):
        return pl.ds(2 * q * W, 2 * W)

    def split_store(ref, first, value, q=0):
        high, low = halves(value)
        ref[pl.ds(first, value.shape[0]), pl.ds(2 * q * W, W)] = high
        ref[pl.ds(first, value.shape[0]), pl.ds((2 * q + 1) * W, W)] = low

    def merged(wide, q=0):
        return wide[:, 2 * q * W : (2 * q + 1) * W] + wide[:, (2 * q + 1) * W : (2 * q + 2) * W]

    inputs = []
    for k, (source, target) in enumerate(zip((map_ref, face_ref, wave_ref, ops_ref), (w.map, w.face, w.wave, w.ops))):
        inputs.append(pltpu.make_async_copy(source, target, w.input_sem.at[k]))
        inputs[k].start()
    greet()
    map_ref, face_ref, wave_ref = w.map, w.face, w.wave
    inputs[0].wait()
    inputs[1].wait()

    w.index[...] = jnp.full(w.index.shape, -1.0, f32)
    w.index[pl.ds(0, C), pl.ds(0, s.nodes)] = map_ref[...].astype(f32)
    w.index[pl.ds(C, 1), pl.ds(0, s.face)] = face_ref[...].astype(f32)
    columns = jnp.transpose(w.index[...])

    def one_hot(match):
        return jnp.where(match, 1.0, 0.0).astype(bf16)

    def iota(shape, axis):
        return lax.broadcasted_iota(jnp.int32, shape, axis).astype(f32)

    faces = columns[: s.face, C : C + 1]
    w.face_rows[...] = one_hot(faces == iota((s.face, s.own_pad), 1))
    w.vec[pl.ds(s.own, s.depth - s.own), :] = jnp.zeros((s.depth - s.own, w.vec.shape[1]), bf16)
    inputs[2].wait()
    for q in blocks:
        split_store(w.vec, 0, wave_ref[:, pl.ds(q * W, W)], q)
    lower = dot(w.face_rows[...], w.vec[pl.ds(0, s.own_pad), :])
    for q in blocks:
        w.face_send[q] = merged(lower, q)

    def remote(send, recv, send_sem, recv_sem, target):
        return pltpu.make_async_remote_copy(
            src_ref=send, dst_ref=recv, send_sem=send_sem, recv_sem=recv_sem,
            device_id={"dom": target}, device_id_type=MESH)

    def face_copy(q):
        return remote(w.face_send.at[q], w.face_recv.at[q], w.face_ssem.at[q], w.face_rsem.at[q], left)

    def back_copy(step, q):
        return remote(w.back_send.at[step, q], w.back_recv.at[step, q],
                      w.back_ssem.at[step, q], w.back_rsem.at[step, q], right)

    def edge_copy(step, q):
        return remote(w.edge_send.at[step, q], w.edge_recv.at[step, q],
                      w.edge_ssem.at[step, q], w.edge_rsem.at[step, q], left)

    def setup_take():
        for c in range(C):
            w.take[pl.ds(c * R, R), :] = one_hot(columns[:R, c : c + 1] == iota((R, s.depth), 1))

    def setup_ops():
        w.op_pad[...] = jnp.zeros(w.op_pad.shape, f32)
        inputs[3].wait()
        for c in range(C):
            w.op_pad[c, pl.ds(0, s.nodes), pl.ds(0, s.nodes)] = w.ops[:, c, :]
            high, low = halves(w.op_pad[c])
            w.op_high[c] = high
            w.op_low[c] = low

    def setup_put():
        for c in range(C):
            row = w.index[c : c + 1, pl.ds(0, L)]
            w.put[pl.ds(0, known), pl.ds(c * L, L)] = one_hot(row == iota((known, L), 0))
            w.put[pl.ds(known, s.face), pl.ds(c * L, L)] = one_hot(row == faces)
            if L > R:
                w.prod[pl.ds(c * L + R, L - R), :] = jnp.zeros((L - R, w.prod.shape[1]), bf16)
                w.cell[c, pl.ds(R, L - R), :] = jnp.zeros((L - R, 2 * W), bf16)
        w.put_back[...] = one_hot(w.index[C : C + 1, pl.ds(0, s.face_pad)] == iota((s.own, s.face_pad), 0))
        for q in range(s.blocks):
            w.far[q] = jnp.zeros(w.far.shape[1:], bf16)
            if s.face_pad > s.face:
                w.back[q, pl.ds(s.face, s.face_pad - s.face), :] = jnp.zeros((s.face_pad - s.face, 2 * W), bf16)

    def gather():
        w.part[...] = dot(w.take[:, pl.ds(0, s.own_pad)], w.vec[pl.ds(0, s.own_pad), :])

    def middle(step, q):
        last = step == DEGREE - 1
        if step == 0:
            face_copy(q).wait()
            split_store(w.far.at[q], s.own - s.base, w.face_recv[q])
        for c in range(C):
            rows = pl.ds(c * R, R)
            if step == 0:
                cell = w.part[rows, span(q)] + dot(w.take[rows, pl.ds(s.base, s.depth - s.base)], w.far[q])
            else:
                cell = dot(w.take[rows, :], w.vec[:, span(q)])
            w.cell[c, pl.ds(0, R), :] = cell.astype(bf16)
        for c in range(C):
            wide = dot(w.op_high[c], w.cell[c])
            value = wide[:, :W] + wide[:, W:] + dot(w.op_low[c], w.cell[c, :, pl.ds(0, W)])
            split_store(w.prod, c * L, value, q)
        count = s.face if last else 2 * s.face
        tail = merged(dot(w.put[pl.ds(s.own, count), :], w.prod[:, span(q)]))
        w.back_send[step, q] = tail[: s.face]
        back_copy(step, q).start()
        if not last:
            w.edge_send[step, q] = tail[s.face :]
            edge_copy(step, q).start()

    def scatter():
        wide = dot(w.put[pl.ds(0, s.own), :], w.prod[...])
        for q in blocks:
            w.applied[q] = merged(wide, q)

    def advance(step, applied, current, earlier):
        if step == 0:
            return (applied - cheb_centre * current) / cheb_half
        return 2.0 * (applied - cheb_centre * current) / cheb_half - earlier

    def finish(step, q):
        back_copy(step, q).wait()
        split_store(w.back.at[q], 0, w.back_recv[step, q])
        applied = w.applied[q] + merged(dot(w.put_back[...], w.back[q]))
        columns = pl.ds(q * W, W)

        def stage(k):
            return wave_ref[:, columns] if k == 0 else w.stages[k - 1, :, columns]

        following = advance(step, applied, stage(step), stage(step - 1) if step else None)
        if step == DEGREE - 1:
            result_ref[:, columns] = following
            done(q)
            return
        w.stages[step, :, columns] = following
        split_store(w.vec, 0, following, q)
        edge_copy(step, q).wait()

        def edge(k):
            return w.face_recv[q] if k == 0 else w.edges[k - 1, q]

        outer = advance(step, w.back_send[step, q] + w.edge_recv[step, q], edge(step), edge(step - 1) if step else None)
        w.edges[step, q] = outer
        split_store(w.vec, s.own, outer, q)

    setup_take()
    setup_ops()
    setup_put()
    ready()
    for q in blocks:
        face_copy(q).start()
    gather()
    for q in blocks:
        middle(0, q)
    scatter()
    for step in range(1, DEGREE):
        for q in blocks:
            finish(step - 1, q)
            middle(step, q)
        scatter()
    for q in blocks:
        finish(DEGREE - 1, q)


def band_copy(s, band_ref, w, turn, first, q):
    half = s.own // 2
    rows = pl.ds(pl.multiple_of(first * half, 8), half)
    columns = pl.ds(q * s.block, s.block)
    return pltpu.make_async_remote_copy(
        src_ref=band_ref.at[rows, columns], dst_ref=w.far_band.at[rows, columns],
        send_sem=w.band_ssem.at[turn, q], recv_sem=w.band_rsem.at[turn, q],
        device_id={"band": 1 - lax.axis_index("band")}, device_id_type=MESH)


def gram_steps(s, band_ref, out_ref, w):
    me = lax.axis_index("dom")
    band = lax.axis_index("band")
    other = 1 - band
    chip, core = me // 2, lax.rem(me, 2)
    partner = chip * 2 + (1 - core)
    W, half, n, chunk = s.width, s.own // 2, s.chips, s.chunk

    def core_copy(m):
        return pltpu.make_async_remote_copy(
            src_ref=w.sums.at[m, 1 - core], dst_ref=w.core_recv.at[m],
            send_sem=w.core_ssem.at[m], recv_sem=w.core_rsem.at[m],
            device_id={"dom": partner}, device_id_type=MESH)

    def scatter_copies(m):
        copies = []
        for j in range(1, n):
            target = lax.rem(chip + j, n)
            copies.append(pltpu.make_async_remote_copy(
                src_ref=w.pair.at[m, target], dst_ref=w.scat_recv.at[m, j - 1],
                send_sem=w.scat_ssem.at[m, j - 1], recv_sem=w.scat_rsem.at[m, j - 1],
                device_id={"dom": target * 2 + core}, device_id_type=MESH))
        return copies

    def gather_copies(m):
        copies = []
        for j in range(1, n):
            target = lax.rem(chip + j, n)
            copies.append(pltpu.make_async_remote_copy(
                src_ref=w.full.at[m, core, chip], dst_ref=w.full.at[m, core, chip],
                send_sem=w.gath_ssem.at[m, j - 1], recv_sem=w.gath_rsem.at[m, j - 1],
                device_id={"dom": target * 2 + core}, device_id_type=MESH))
        return copies

    def swap_copy(m):
        return pltpu.make_async_remote_copy(
            src_ref=w.full.at[m, core], dst_ref=w.full.at[m, core],
            send_sem=w.swap_ssem.at[m], recv_sem=w.swap_rsem.at[m],
            device_id={"dom": partner}, device_id_type=MESH)

    def cross_copy():
        return pltpu.make_async_remote_copy(
            src_ref=w.cross_send, dst_ref=w.cross_recv,
            send_sem=w.cross_ssem, recv_sem=w.cross_rsem,
            device_id={"band": other}, device_id_type=MESH)

    def norm_copy():
        return pltpu.make_async_remote_copy(
            src_ref=w.norm_send, dst_ref=w.norm_recv,
            send_sem=w.norm_ssem, recv_sem=w.norm_rsem,
            device_id={"band": other}, device_id_type=MESH)

    def put_sums(m, value):
        w.sums[m] = value.reshape(2, W // 2, W)

    def pair_up(m):
        core_copy(m).wait()
        total = w.sums[m, core] + w.core_recv[m]
        w.pair[m] = total.reshape(n, chunk, W)

    def own_total(m):
        wait_all(scatter_copies(m))
        total = w.pair[m, chip]
        for j in range(n - 1):
            total = total + w.scat_recv[m, j]
        return total

    high, low = halves(band_ref[...])
    def fill(ref, value):
        count, size = value.shape[0], ref.shape[0]
        ref[pl.ds(0, count), :] = value
        if size > count:
            ref[pl.ds(count, size - count), :] = jnp.zeros((size - count, W), bf16)

    fill(w.near_high, high)
    fill(w.near_low, low)
    turned_high, turned_low = halves(jnp.transpose(w.bands[...]))
    put_sums(0, dot(turned_high, w.near_high[...])
             + dot(turned_high, w.near_low[...])
             + dot(turned_low, w.near_high[...]))
    core_copy(0).start()
    pair_up(0)
    start_all(scatter_copies(0))
    same = own_total(0)
    w.full[0, core, chip] = same
    start_all(gather_copies(0))

    for q in range(s.blocks):
        band_copy(s, band_ref, w, 0, other, q).wait_send()
        band_copy(s, band_ref, w, 0, band, q).wait_recv()
    rows = pl.ds(pl.multiple_of(band * half, 16), half)
    far_high, far_low = halves(w.far_band[rows, :])
    near_high, near_low = w.near_high[rows, :], w.near_low[rows, :]
    first = band == 0

    def pick(a, b):
        return jnp.where(first, a, b)

    fill(w.left_high, pick(far_high, near_high))
    fill(w.left_low, pick(far_low, near_low))
    fill(w.right_high, pick(near_high, far_high))
    fill(w.right_low, pick(near_low, far_low))
    put_sums(1, dot_tn(w.left_high[...], w.right_high[...])
             + dot_tn(w.left_high[...], w.right_low[...])
             + dot_tn(w.left_low[...], w.right_high[...]))
    core_copy(1).start()
    band_copy(s, band_ref, w, 1, band, 0).start()
    pair_up(1)
    start_all(scatter_copies(1))

    wait_all(gather_copies(0))
    swap_copy(0).start()
    cross = own_total(1)
    w.cross_send[...] = cross
    cross_copy().start()
    for q in range(1, s.blocks):
        band_copy(s, band_ref, w, 1, band, q).start()
    swap_copy(0).wait()
    near_block = w.full[0].reshape(W, W)

    def squares(value):
        return (value * value).reshape(W // 8, 8, W).sum(0)

    near_squares = squares(near_block)
    w.norm_send[...] = near_squares
    norm_copy().start()
    block_high, block_low = halves(near_block)
    w.block_high[0] = block_high
    w.block_low[0] = block_low
    cross_copy().wait()
    cross = pick(cross, w.cross_recv[...]) + pick(w.cross_recv[...], cross)
    w.full[1, core, chip] = cross
    start_all(gather_copies(1))
    near_high, near_low = w.near_high[pl.ds(0, s.own), :], w.near_low[pl.ds(0, s.own), :]
    near_wide = dot(near_high, w.block_high[0]) + dot(near_high, w.block_low[0])
    w.near_prod[...] = near_wide + dot(near_low, w.block_high[0])
    for q in range(s.blocks):
        band_copy(s, band_ref, w, 1, band, q).wait_send()
        band_copy(s, band_ref, w, 1, other, q).wait_recv()
    high, low = halves(w.far_band[...])
    w.far_high[...] = high
    w.far_low[...] = low
    wait_all(gather_copies(1))
    swap_copy(1).start()
    swap_copy(1).wait()
    norm_copy().wait()
    far_block = w.full[1].reshape(W, W)
    total = jnp.sum(near_squares + w.norm_recv[...] + 2.0 * squares(far_block))
    norm = jnp.sqrt(jnp.full((1, W), total, f32) + 1e-06)
    far_block = pick(far_block, jnp.transpose(far_block))
    block_high, block_low = halves(far_block)
    w.block_high[1] = block_high
    w.block_low[1] = block_low
    wide = dot(w.far_high[...], w.block_high[1]) + dot(w.far_high[...], w.block_low[1])
    wide = wide + dot(w.far_low[...], w.block_high[1]) + w.near_prod[...]
    out_ref[...] = 1.5 * band_ref[...] - wide * (0.5 / norm)


def kernel(s, names, wave_ref, ops_ref, map_ref, face_ref, out_ref, *scratch):
    w = types.SimpleNamespace(**dict(zip(names, scratch)))
    me = lax.axis_index("dom")
    barrier = pltpu.get_barrier_semaphore()
    greeted = [{"dom": lax.rem(me + 1, s.n_dom)}, {"dom": lax.rem(me + s.n_dom - 1, s.n_dom)}]
    if s.gram:
        chip, core = me // 2, lax.rem(me, 2)
        greeted.append({"dom": chip * 2 + (1 - core)})
        greeted.append({"band": 1 - lax.axis_index("band")})
        for j in range(1, s.chips):
            greeted.append({"dom": lax.rem(chip + j, s.chips) * 2 + core})

    def greet():
        for device in greeted:
            pl.semaphore_signal(barrier, inc=1, device_id=device, device_id_type=MESH)

    def ready():
        pl.semaphore_wait(barrier, len(greeted))

    if s.gram:
        if s.own_pad > s.own:
            w.bands[pl.ds(s.own, s.own_pad - s.own), :] = jnp.zeros((s.own_pad - s.own, s.width), f32)
        owned = w.bands.at[pl.ds(0, s.own), :]

        def send(q):
            band_copy(s, owned, w, 0, 1 - lax.axis_index("band"), q).start()

        filter_steps(s, greet, ready, send, wave_ref, ops_ref, map_ref, face_ref, owned, w)
        gram_steps(s, owned, out_ref, w)
    else:
        filter_steps(s, greet, ready, lambda q: None, wave_ref, ops_ref, map_ref, face_ref, out_ref, w)


def scratch_of(s):
    C, R, L, W, n, chunk = s.cells, s.rows, s.lanes, s.width, s.chips, s.chunk
    V, dma = pltpu.VMEM, pltpu.SemaphoreType.DMA
    scratch = dict(
        index=V((128, max(L, s.face_pad)), f32),
        face_rows=V((s.face, s.own_pad), bf16),
        vec=V((s.depth, 2 * W), bf16),
        take=V((C * R, s.depth), bf16),
        put=V((s.own + 2 * s.face, C * L), bf16),
        put_back=V((s.own, s.face_pad), bf16),
        ops=V((s.nodes, C, s.nodes), f32),
        map=V((C, s.nodes), jnp.int32),
        face=V((1, s.face), jnp.int32),
        wave=V((s.own, W), f32),
        input_sem=dma((4,)),
        op_pad=V((C, R, L), f32),
        op_high=V((C, R, L), bf16),
        op_low=V((C, R, L), bf16),
        part=V((C * R, 2 * W), f32),
        applied=V((s.blocks, s.own, s.block), f32),
        cell=V((C, L, 2 * s.block), bf16),
        prod=V((C * L, 2 * W), bf16),
        far=V((s.blocks, s.depth - s.base, 2 * s.block), bf16),
        back=V((s.blocks, s.face_pad, 2 * s.block), bf16),
        stages=V((DEGREE - 1, s.own, W), f32),
        edges=V((DEGREE - 1, s.blocks, s.face, s.block), f32),
        face_send=V((s.blocks, s.face, s.block), f32),
        face_recv=V((s.blocks, s.face, s.block), f32),
        edge_send=V((DEGREE - 1, s.blocks, s.face, s.block), f32),
        edge_recv=V((DEGREE - 1, s.blocks, s.face, s.block), f32),
        back_send=V((DEGREE, s.blocks, s.face, s.block), f32),
        back_recv=V((DEGREE, s.blocks, s.face, s.block), f32),
        face_ssem=dma((s.blocks,)),
        face_rsem=dma((s.blocks,)),
        edge_ssem=dma((DEGREE - 1, s.blocks)),
        edge_rsem=dma((DEGREE - 1, s.blocks)),
        back_ssem=dma((DEGREE, s.blocks)),
        back_rsem=dma((DEGREE, s.blocks)),
    )
    if s.gram:
        scratch |= dict(
            bands=V((s.own_pad, W), f32),
            far_band=V((s.own, W), f32),
            near_high=V((s.own_pad, W), bf16),
            near_low=V((s.own_pad, W), bf16),
            left_high=V((s.half_pad, W), bf16),
            left_low=V((s.half_pad, W), bf16),
            right_high=V((s.half_pad, W), bf16),
            right_low=V((s.half_pad, W), bf16),
            far_high=V((s.own, W), bf16),
            far_low=V((s.own, W), bf16),
            near_prod=V((s.own, W), f32),
            block_high=V((2, W, W), bf16),
            block_low=V((2, W, W), bf16),
            sums=V((2, 2, W // 2, W), f32),
            core_recv=V((2, W // 2, W), f32),
            pair=V((2, n, chunk, W), f32),
            scat_recv=V((2, n - 1, chunk, W), f32),
            full=V((2, 2, n, chunk, W), f32),
            cross_send=V((chunk, W), f32),
            cross_recv=V((chunk, W), f32),
            norm_send=V((8, W), f32),
            norm_recv=V((8, W), f32),
            norm_ssem=dma,
            norm_rsem=dma,
            cross_ssem=dma,
            cross_rsem=dma,
            band_ssem=dma((2, s.blocks)),
            band_rsem=dma((2, s.blocks)),
            core_ssem=dma((2,)),
            core_rsem=dma((2,)),
            swap_ssem=dma((2,)),
            swap_rsem=dma((2,)),
            scat_ssem=dma((2, n - 1)),
            scat_rsem=dma((2, n - 1)),
            gath_ssem=dma((2, n - 1)),
            gath_rsem=dma((2, n - 1)),
        )
    return scratch


def on_device(wavefun, cell_ops, cell_map, face_list):
    s = Sizes(lax.axis_size("dom"), lax.axis_size("band"), wavefun.shape[0], wavefun.shape[1],
              cell_map.shape[0], cell_map.shape[1], face_list.shape[0])
    scratch = scratch_of(s)
    latest = pl.pallas_call(
        functools.partial(kernel, s, list(scratch)),
        out_shape=jax.ShapeDtypeStruct(wavefun.shape, f32),
        in_specs=[pl.BlockSpec(memory_space=space) for space in (pl.ANY,) * 4],
        out_specs=pl.BlockSpec(memory_space=pltpu.VMEM),
        scratch_shapes=list(scratch.values()),
        compiler_params=pltpu.CompilerParams(
            collective_id=0, has_side_effects=True, vmem_limit_bytes=60 * 1024 * 1024),
        name="filtered_bands",
    )(wavefun, jnp.swapaxes(cell_ops, 0, 1), cell_map, face_list.reshape(1, -1))
    if s.gram:
        return latest
    full_bands = lax.all_gather(latest, "band", axis=1, tiled=True)
    partial_value = jnp.einsum("nb,nc->bc", full_bands, full_bands, precision=lax.Precision.HIGHEST)
    margin = lax.psum(partial_value, "dom")
    norm_value = jnp.sqrt(jnp.sum(margin * margin) + 1e-06)
    full_width = margin.shape[0]
    offset = lax.axis_index("band") * s.width
    scaled_cols = lax.dynamic_slice_in_dim(margin, offset, s.width, 1) / norm_value
    identity_cols = lax.dynamic_slice_in_dim(
        jnp.eye(full_width, dtype=jnp.float32), offset, s.width, 1
    )
    mixing = (3.0 * identity_cols - scaled_cols) / 2.0
    return jnp.dot(full_bands, mixing, precision=lax.Precision.HIGHEST)


def solution(mesh):
    return jax.shard_map(
        on_device,
        mesh=mesh,
        in_specs=(P("dom", "band"), P("dom", None, None), P("dom", None), P("dom")),
        out_specs=P("dom", "band"),
        check_vma=False,
    )
```

```python
import functools
import types

import jax
import jax.numpy as jnp
from jax import lax
from jax.experimental import pallas as pl
from jax.experimental.pallas import tpu as pltpu
from jax.sharding import PartitionSpec as P

DEGREE = 2


cheb_centre = 1.0
cheb_half = 1.6

f32 = jnp.float32
bf16 = jnp.bfloat16
MESH = pl.DeviceIdType.MESH
VMEM_LIMIT = 58 * 1024 * 1024


def round_up(value, step):
    return (value + step - 1) // step * step


def halves(value):
    high = value.astype(bf16)
    low = (value - high.astype(f32)).astype(bf16)
    return high, low


def dot(left, right):
    return jnp.dot(left, right, preferred_element_type=f32)


def dot_tn(left, right):
    return lax.dot_general(left, right, (((0,), (0,)), ((), ())), preferred_element_type=f32)


def dot_nt(left, right):
    return lax.dot_general(left, right, (((1,), (1,)), ((), ())), preferred_element_type=f32)


class Sizes:
    def __init__(self, n_dom, n_band, own, width, cells, nodes, face):
        self.n_dom, self.n_band = n_dom, n_band
        self.own, self.width = own, width
        self.cells, self.nodes, self.face = cells, nodes, face
        self.own_pad = round_up(own, 128)
        self.face_pad = round_up(face, 128)
        self.rows = round_up(nodes, 16)
        self.lanes = round_up(nodes, 128)
        self.blocks = 2 if width % 256 == 0 else 1
        self.block = width // self.blocks
        self.depth = round_up(own + face, 128)
        self.base = own // 128 * 128
        self.half_pad = round_up(own // 2, 128)
        self.pieces = 3 if own % 48 == 0 else 1
        self.chips = n_dom // 2
        self.chunk = width // n_dom
        self.gram = (
            n_band == 2
            and n_dom % 2 == 0
            and n_dom > 2
            and width % (8 * n_dom) == 0
            and width % 128 == 0
            and own % 32 == 0
        )


def start_all(copies):
    for copy in copies:
        copy.start()


def wait_all(copies):
    for copy in copies:
        copy.wait()


def filter_steps(s, greet, ready, done, wave_ref, ops_ref, map_ref, face_ref, result_ref, w):
    me = lax.axis_index("dom")
    right = lax.rem(me + 1, s.n_dom)
    left = lax.rem(me + s.n_dom - 1, s.n_dom)
    C, R, L, W = s.cells, s.rows, s.lanes, s.block
    known = s.own + s.face
    blocks = range(s.blocks)

    def span(q):
        return pl.ds(2 * q * W, 2 * W)

    def split_store(ref, first, value, q=0):
        high, low = halves(value)
        ref[pl.ds(first, value.shape[0]), pl.ds(2 * q * W, W)] = high
        ref[pl.ds(first, value.shape[0]), pl.ds((2 * q + 1) * W, W)] = low

    def merged(wide, q=0):
        return wide[:, 2 * q * W : (2 * q + 1) * W] + wide[:, (2 * q + 1) * W : (2 * q + 2) * W]

    inputs = []
    for k, (source, target) in enumerate(zip((map_ref, face_ref, wave_ref, ops_ref), (w.map, w.face, w.wave, w.ops))):
        inputs.append(pltpu.make_async_copy(source, target, w.input_sem.at[k]))
        inputs[k].start()
    greet()
    map_ref, face_ref, wave_ref = w.map, w.face, w.wave
    inputs[0].wait()
    inputs[1].wait()

    w.index[...] = jnp.full(w.index.shape, -1.0, f32)
    w.index[pl.ds(0, C), pl.ds(0, s.nodes)] = map_ref[...].astype(f32)
    w.index[pl.ds(C, 1), pl.ds(0, s.face)] = face_ref[...].astype(f32)
    columns = jnp.transpose(w.index[...])

    def one_hot(match):
        return jnp.where(match, 1.0, 0.0).astype(bf16)

    def iota(shape, axis):
        return lax.broadcasted_iota(jnp.int32, shape, axis).astype(f32)

    faces = columns[: s.face, C : C + 1]
    w.face_rows[...] = one_hot(faces == iota((s.face, s.own_pad), 1))
    w.vec[pl.ds(s.own, s.depth - s.own), :] = jnp.zeros((s.depth - s.own, w.vec.shape[1]), bf16)
    inputs[2].wait()
    for q in blocks:
        split_store(w.vec, 0, wave_ref[:, pl.ds(q * W, W)], q)
    lower = dot(w.face_rows[...], w.vec[pl.ds(0, s.own_pad), :])
    for q in blocks:
        w.face_send[q] = merged(lower, q)

    def remote(send, recv, send_sem, recv_sem, target):
        return pltpu.make_async_remote_copy(
            src_ref=send, dst_ref=recv, send_sem=send_sem, recv_sem=recv_sem,
            device_id={"dom": target}, device_id_type=MESH)

    def face_copy(q):
        return remote(w.face_send.at[q], w.face_recv.at[q], w.face_ssem.at[q], w.face_rsem.at[q], left)

    def back_copy(step, q):
        return remote(w.back_send.at[step, q], w.back_recv.at[step, q],
                      w.back_ssem.at[step, q], w.back_rsem.at[step, q], right)

    def edge_copy(step, q):
        return remote(w.edge_send.at[step, q], w.edge_recv.at[step, q],
                      w.edge_ssem.at[step, q], w.edge_rsem.at[step, q], left)

    def setup_take():
        for c in range(C):
            w.take[pl.ds(c * R, R), :] = one_hot(columns[:R, c : c + 1] == iota((R, s.depth), 1))

    def setup_ops():
        w.op_pad[...] = jnp.zeros(w.op_pad.shape, f32)
        inputs[3].wait()
        for c in range(C):
            w.op_pad[c, pl.ds(0, s.nodes), pl.ds(0, s.nodes)] = w.ops[:, c, :]
            high, low = halves(w.op_pad[c])
            w.op_high[c] = high
            w.op_low[c] = low

    def setup_put():
        for c in range(C):
            row = w.index[c : c + 1, pl.ds(0, L)]
            w.put[pl.ds(0, known), pl.ds(c * L, L)] = one_hot(row == iota((known, L), 0))
            w.put[pl.ds(known, s.face), pl.ds(c * L, L)] = one_hot(row == faces)
            if L > R:
                w.prod[pl.ds(c * L + R, L - R), :] = jnp.zeros((L - R, w.prod.shape[1]), bf16)
                w.cell[c, pl.ds(R, L - R), :] = jnp.zeros((L - R, 2 * W), bf16)
        w.put_back[...] = one_hot(w.index[C : C + 1, pl.ds(0, s.face_pad)] == iota((s.own, s.face_pad), 0))
        for q in range(s.blocks):
            w.far[q] = jnp.zeros(w.far.shape[1:], bf16)
            if s.face_pad > s.face:
                w.back[q, pl.ds(s.face, s.face_pad - s.face), :] = jnp.zeros((s.face_pad - s.face, 2 * W), bf16)

    def gather():
        w.part[...] = dot(w.take[:, pl.ds(0, s.own_pad)], w.vec[pl.ds(0, s.own_pad), :])

    def middle(step, q):
        last = step == DEGREE - 1
        if step == 0:
            face_copy(q).wait()
            split_store(w.far.at[q], s.own - s.base, w.face_recv[q])
        for c in range(C):
            rows = pl.ds(c * R, R)
            if step == 0:
                cell = w.part[rows, span(q)] + dot(w.take[rows, pl.ds(s.base, s.depth - s.base)], w.far[q])
            else:
                cell = dot(w.take[rows, :], w.vec[:, span(q)])
            w.cell[c, pl.ds(0, R), :] = cell.astype(bf16)
        for c in range(C):
            wide = dot(w.op_high[c], w.cell[c])
            value = wide[:, :W] + wide[:, W:] + dot(w.op_low[c], w.cell[c, :, pl.ds(0, W)])
            split_store(w.prod, c * L, value, q)
        count = s.face if last else 2 * s.face
        tail = merged(dot(w.put[pl.ds(s.own, count), :], w.prod[:, span(q)]))
        w.back_send[step, q] = tail[: s.face]
        back_copy(step, q).start()
        if not last:
            w.edge_send[step, q] = tail[s.face :]
            edge_copy(step, q).start()

    def scatter():
        wide = dot(w.put[pl.ds(0, s.own), :], w.prod[...])
        for q in blocks:
            w.applied[q] = merged(wide, q)

    def advance(step, applied, current, earlier):
        if step == 0:
            return (applied - cheb_centre * current) / cheb_half
        return 2.0 * (applied - cheb_centre * current) / cheb_half - earlier

    def finish(step, q):
        back_copy(step, q).wait()
        split_store(w.back.at[q], 0, w.back_recv[step, q])
        applied = w.applied[q] + merged(dot(w.put_back[...], w.back[q]))
        columns = pl.ds(q * W, W)

        def stage(k):
            return wave_ref[:, columns] if k == 0 else w.stages[k - 1, :, columns]

        following = advance(step, applied, stage(step), stage(step - 1) if step else None)
        if step == DEGREE - 1:
            result_ref[:, columns] = following
            done(q)
            return
        w.stages[step, :, columns] = following
        split_store(w.vec, 0, following, q)
        edge_copy(step, q).wait()

        def edge(k):
            return w.face_recv[q] if k == 0 else w.edges[k - 1, q]

        outer = advance(step, w.back_send[step, q] + w.edge_recv[step, q], edge(step), edge(step - 1) if step else None)
        w.edges[step, q] = outer
        split_store(w.vec, s.own, outer, q)

    setup_take()
    setup_ops()
    setup_put()
    ready()
    for q in blocks:
        face_copy(q).start()
    gather()
    for q in blocks:
        middle(0, q)
    scatter()
    for step in range(1, DEGREE):
        for q in blocks:
            finish(step - 1, q)
            middle(step, q)
        scatter()
    for q in blocks:
        finish(DEGREE - 1, q)


def band_copy(s, band_ref, w, turn, first, q):
    half = s.own // 2
    if turn:
        size = half // s.pieces
        rows = pl.ds(pl.multiple_of(first * half + q * size, 8), size)
        columns = pl.ds(0, s.width)
    else:
        rows = pl.ds(pl.multiple_of(first * half, 8), half)
        columns = pl.ds(q * s.block, s.block)
    return pltpu.make_async_remote_copy(
        src_ref=band_ref.at[rows, columns], dst_ref=w.far_band.at[rows, columns],
        send_sem=w.band_ssem.at[turn, q], recv_sem=w.band_rsem.at[turn, q],
        device_id={"band": 1 - lax.axis_index("band")}, device_id_type=MESH)


def gram_steps(s, band_ref, wide_ref, total_ref, w):
    me = lax.axis_index("dom")
    band = lax.axis_index("band")
    other = 1 - band
    chip, core = me // 2, lax.rem(me, 2)
    partner = chip * 2 + (1 - core)
    W, half, n, chunk = s.width, s.own // 2, s.chips, s.chunk

    def core_copy(m):
        return pltpu.make_async_remote_copy(
            src_ref=w.sums.at[m, 1 - core], dst_ref=w.core_recv.at[m],
            send_sem=w.core_ssem.at[m], recv_sem=w.core_rsem.at[m],
            device_id={"dom": partner}, device_id_type=MESH)

    upper = chip * 2 // n

    def farthest(i):
        falling, rising = n - 1 - i, i
        falling = falling - (chip - falling + n) // n
        rising = rising + (rising - chip + n) // n
        return (1 - upper) * falling + upper * rising

    def spread(i, source, target, send_sem, recv_sem):
        chip_to = farthest(i)
        slot = lax.rem(chip_to - chip + n, n) - 1
        return pltpu.make_async_remote_copy(
            src_ref=source(chip_to), dst_ref=target(slot),
            send_sem=send_sem.at[i], recv_sem=recv_sem.at[slot],
            device_id={"dom": chip_to * 2 + core}, device_id_type=MESH)

    def scatter_copies(m):
        return [
            spread(i, lambda t: w.pair.at[m, t], lambda slot: w.scat_recv.at[m, slot], w.scat_ssem.at[m], w.scat_rsem.at[m])
            for i in range(n - 1)
        ]

    def gather_copies(m):
        return [
            spread(i, lambda t: w.full.at[m, core, chip], lambda slot: w.full.at[m, core, chip],
                   w.gath_ssem.at[m], w.gath_rsem.at[m])
            for i in range(n - 1)
        ]

    def swap_copy(m):
        return pltpu.make_async_remote_copy(
            src_ref=w.full.at[m, core], dst_ref=w.full.at[m, core],
            send_sem=w.swap_ssem.at[m], recv_sem=w.swap_rsem.at[m],
            device_id={"dom": partner}, device_id_type=MESH)

    def cross_copy():
        return pltpu.make_async_remote_copy(
            src_ref=w.cross_send, dst_ref=w.cross_recv,
            send_sem=w.cross_ssem, recv_sem=w.cross_rsem,
            device_id={"band": other}, device_id_type=MESH)

    def norm_copy():
        return pltpu.make_async_remote_copy(
            src_ref=w.norm_send, dst_ref=w.norm_recv,
            send_sem=w.norm_ssem, recv_sem=w.norm_rsem,
            device_id={"band": other}, device_id_type=MESH)

    def put_sums(m, value):
        w.sums[m] = value.reshape(2, W // 2, W)

    def pair_up(m):
        core_copy(m).wait()
        total = w.sums[m, core] + w.core_recv[m]
        w.pair[m] = total.reshape(n, chunk, W)

    def own_total(m):
        wait_all(scatter_copies(m))
        total = w.pair[m, chip]
        for j in range(n - 1):
            total = total + w.scat_recv[m, j]
        return total

    owned = band_ref.at[pl.ds(0, s.own), :]
    high, low = halves(owned[...])

    def fill(ref, value):
        count, size = value.shape[0], ref.shape[0]
        ref[pl.ds(0, count), :] = value
        if size > count:
            ref[pl.ds(count, size - count), :] = jnp.zeros((size - count, W), bf16)

    fill(w.near_high, high)
    fill(w.near_low, low)
    turned_high, turned_low = halves(jnp.transpose(band_ref[...]))
    put_sums(0, dot(turned_high, w.near_high[...])
             + dot(turned_high, w.near_low[...])
             + dot(turned_low, w.near_high[...]))
    core_copy(0).start()
    pair_up(0)
    start_all(scatter_copies(0))
    same = own_total(0)
    w.full[0, core, chip] = same
    start_all(gather_copies(0))

    for q in range(s.blocks):
        band_copy(s, owned, w, 0, other, q).wait_send()
        band_copy(s, owned, w, 0, band, q).wait_recv()
    rows = pl.ds(pl.multiple_of(band * half, 16), half)
    far_high, far_low = halves(w.far_band[rows, :])
    near_high, near_low = w.near_high[rows, :], w.near_low[rows, :]
    first = band == 0

    def pick(a, b):
        return jnp.where(first, a, b)

    fill(w.left_high, pick(far_high, near_high))
    fill(w.left_low, pick(far_low, near_low))
    fill(w.right_high, pick(near_high, far_high))
    fill(w.right_low, pick(near_low, far_low))
    put_sums(1, dot_tn(w.left_high[...], w.right_high[...])
             + dot_tn(w.left_high[...], w.right_low[...])
             + dot_tn(w.left_low[...], w.right_high[...]))
    core_copy(1).start()
    for q in range(s.pieces - 1):
        band_copy(s, owned, w, 1, band, q).start()
    pair_up(1)
    start_all(scatter_copies(1))

    wait_all(gather_copies(0))
    swap_copy(0).start()
    cross = own_total(1)
    w.cross_send[...] = cross
    cross_copy().start()
    band_copy(s, owned, w, 1, band, s.pieces - 1).start()
    swap_copy(0).wait()
    near_block = w.full[0].reshape(W, W)

    def squares(value):
        return (value * value).reshape(W // 8, 8, W).sum(0)

    near_squares = squares(near_block)
    w.norm_send[...] = near_squares
    norm_copy().start()
    block_high, block_low = halves(near_block)
    w.block_high[0] = block_high
    w.block_low[0] = block_low
    cross_copy().wait()
    cross = pick(cross, w.cross_recv[...]) + pick(w.cross_recv[...], cross)
    w.full[1, core, chip] = cross
    start_all(gather_copies(1))
    near_high, near_low = w.near_high[pl.ds(0, s.own), :], w.near_low[pl.ds(0, s.own), :]
    near_wide = dot(near_high, w.block_high[0]) + dot(near_high, w.block_low[0])
    w.near_prod[...] = near_wide + dot(near_low, w.block_high[0])
    for q in range(s.pieces):
        band_copy(s, owned, w, 1, band, q).wait_send()
        band_copy(s, owned, w, 1, other, q).wait_recv()
    high, low = halves(w.far_band[...])
    w.far_high[...] = high
    w.far_low[...] = low
    wait_all(gather_copies(1))
    swap_copy(1).start()
    swap_copy(1).wait()
    norm_copy().wait()
    far_block = w.full[1].reshape(W, W)
    total_ref[...] = near_squares + w.norm_recv[...] + 2.0 * squares(far_block)
    far_block = pick(far_block, jnp.transpose(far_block))
    block_high, block_low = halves(far_block)
    w.block_high[1] = block_high
    w.block_low[1] = block_low
    wide = dot(w.far_high[...], w.block_high[1]) + dot(w.far_high[...], w.block_low[1])
    wide_ref[...] = wide + dot(w.far_low[...], w.block_high[1]) + w.near_prod[...]


def settle_kernel(s, wide_ref, band_ref, total_ref, out_ref, stage, sem):
    norm = jnp.sqrt(jnp.full((1, s.width), jnp.sum(total_ref[...]), f32) + 1e-06)
    scale = 0.5 / norm
    size = s.own // 4
    copies = []
    for k in range(4):
        rows = pl.ds(k * size, size)
        stage[rows, :] = 1.5 * band_ref[rows, :] - wide_ref[rows, :] * scale
        copies.append(pltpu.make_async_copy(stage.at[rows, :], out_ref.at[rows, :], sem.at[k]))
        copies[k].start()
    wait_all(copies)


def kernel(s, names, wave_ref, ops_ref, map_ref, face_ref, *refs):
    outs, scratch = refs[: len(refs) - len(names)], refs[len(refs) - len(names) :]
    w = types.SimpleNamespace(**dict(zip(names, scratch)))
    me = lax.axis_index("dom")
    barrier = pltpu.get_barrier_semaphore()
    greeted = [{"dom": lax.rem(me + 1, s.n_dom)}, {"dom": lax.rem(me + s.n_dom - 1, s.n_dom)}]
    if s.gram:
        chip, core = me // 2, lax.rem(me, 2)
        greeted.append({"dom": chip * 2 + (1 - core)})
        greeted.append({"band": 1 - lax.axis_index("band")})
        for j in range(1, s.chips):
            greeted.append({"dom": lax.rem(chip + j, s.chips) * 2 + core})

    def greet():
        for device in greeted:
            pl.semaphore_signal(barrier, inc=1, device_id=device, device_id_type=MESH)

    def ready():
        pl.semaphore_wait(barrier, len(greeted))

    if s.gram:
        wide_ref, band_ref, total_ref = outs
        if s.own_pad > s.own:
            band_ref[pl.ds(s.own, s.own_pad - s.own), :] = jnp.zeros((s.own_pad - s.own, s.width), f32)
        owned = band_ref.at[pl.ds(0, s.own), :]

        def send(q):
            band_copy(s, owned, w, 0, 1 - lax.axis_index("band"), q).start()

        filter_steps(s, greet, ready, send, wave_ref, ops_ref, map_ref, face_ref, owned, w)
        gram_steps(s, band_ref, wide_ref, total_ref, w)
    else:
        filter_steps(s, greet, ready, lambda q: None, wave_ref, ops_ref, map_ref, face_ref, outs[0], w)


def scratch_of(s):
    C, R, L, W, n, chunk = s.cells, s.rows, s.lanes, s.width, s.chips, s.chunk
    V, dma = pltpu.VMEM, pltpu.SemaphoreType.DMA
    scratch = dict(
        index=V((128, max(L, s.face_pad)), f32),
        face_rows=V((s.face, s.own_pad), bf16),
        vec=V((s.depth, 2 * W), bf16),
        take=V((C * R, s.depth), bf16),
        put=V((s.own + 2 * s.face, C * L), bf16),
        put_back=V((s.own, s.face_pad), bf16),
        ops=V((s.nodes, C, s.nodes), f32),
        map=V((C, s.nodes), jnp.int32),
        face=V((1, s.face), jnp.int32),
        wave=V((s.own, W), f32),
        input_sem=dma((4,)),
        op_pad=V((C, R, L), f32),
        op_high=V((C, R, L), bf16),
        op_low=V((C, R, L), bf16),
        part=V((C * R, 2 * W), f32),
        applied=V((s.blocks, s.own, s.block), f32),
        cell=V((C, L, 2 * s.block), bf16),
        prod=V((C * L, 2 * W), bf16),
        far=V((s.blocks, s.depth - s.base, 2 * s.block), bf16),
        back=V((s.blocks, s.face_pad, 2 * s.block), bf16),
        stages=V((DEGREE - 1, s.own, W), f32),
        edges=V((DEGREE - 1, s.blocks, s.face, s.block), f32),
        face_send=V((s.blocks, s.face, s.block), f32),
        face_recv=V((s.blocks, s.face, s.block), f32),
        edge_send=V((DEGREE - 1, s.blocks, s.face, s.block), f32),
        edge_recv=V((DEGREE - 1, s.blocks, s.face, s.block), f32),
        back_send=V((DEGREE, s.blocks, s.face, s.block), f32),
        back_recv=V((DEGREE, s.blocks, s.face, s.block), f32),
        face_ssem=dma((s.blocks,)),
        face_rsem=dma((s.blocks,)),
        edge_ssem=dma((DEGREE - 1, s.blocks)),
        edge_rsem=dma((DEGREE - 1, s.blocks)),
        back_ssem=dma((DEGREE, s.blocks)),
        back_rsem=dma((DEGREE, s.blocks)),
    )
    if s.gram:
        scratch |= dict(
            far_band=V((s.own, W), f32),
            near_high=V((s.own_pad, W), bf16),
            near_low=V((s.own_pad, W), bf16),
            left_high=V((s.half_pad, W), bf16),
            left_low=V((s.half_pad, W), bf16),
            right_high=V((s.half_pad, W), bf16),
            right_low=V((s.half_pad, W), bf16),
            far_high=V((s.own, W), bf16),
            far_low=V((s.own, W), bf16),
            near_prod=V((s.own, W), f32),
            block_high=V((2, W, W), bf16),
            block_low=V((2, W, W), bf16),
            sums=V((2, 2, W // 2, W), f32),
            core_recv=V((2, W // 2, W), f32),
            pair=V((2, n, chunk, W), f32),
            scat_recv=V((2, n - 1, chunk, W), f32),
            full=V((2, 2, n, chunk, W), f32),
            cross_send=V((chunk, W), f32),
            cross_recv=V((chunk, W), f32),
            norm_send=V((8, W), f32),
            norm_recv=V((8, W), f32),
            norm_ssem=dma,
            norm_rsem=dma,
            cross_ssem=dma,
            cross_rsem=dma,
            band_ssem=dma((2, max(s.blocks, s.pieces))),
            band_rsem=dma((2, max(s.blocks, s.pieces))),
            core_ssem=dma((2,)),
            core_rsem=dma((2,)),
            swap_ssem=dma((2,)),
            swap_rsem=dma((2,)),
            scat_ssem=dma((2, n - 1)),
            scat_rsem=dma((2, n - 1)),
            gath_ssem=dma((2, n - 1)),
            gath_rsem=dma((2, n - 1)),
        )
    return scratch


def on_device(wavefun, cell_ops, cell_map, face_list):
    s = Sizes(lax.axis_size("dom"), lax.axis_size("band"), wavefun.shape[0], wavefun.shape[1],
              cell_map.shape[0], cell_map.shape[1], face_list.shape[0])
    scratch = scratch_of(s)
    shapes = [wavefun.shape]
    if s.gram:
        shapes += [(s.own_pad, s.width), (8, s.width)]
    inside = pl.BlockSpec(memory_space=pltpu.VMEM)
    outs = pl.pallas_call(
        functools.partial(kernel, s, list(scratch)),
        out_shape=[pltpu.VMEM(shape, f32) if s.gram else jax.ShapeDtypeStruct(shape, f32) for shape in shapes],
        in_specs=[pl.BlockSpec(memory_space=pl.ANY)] * 4,
        out_specs=[inside] * len(shapes),
        scratch_shapes=list(scratch.values()),
        compiler_params=pltpu.CompilerParams(
            collective_id=0, has_side_effects=True, vmem_limit_bytes=VMEM_LIMIT),
        name="filtered_bands",
    )(wavefun, jnp.swapaxes(cell_ops, 0, 1), cell_map, face_list.reshape(1, -1))
    if s.gram:
        return pl.pallas_call(
            functools.partial(settle_kernel, s),
            out_shape=jax.ShapeDtypeStruct(wavefun.shape, f32),
            in_specs=[inside] * 3,
            out_specs=pl.BlockSpec(memory_space=pl.ANY),
            scratch_shapes=[pltpu.VMEM(wavefun.shape, f32), pltpu.SemaphoreType.DMA((4,))],
            compiler_params=pltpu.CompilerParams(vmem_limit_bytes=8 * 1024 * 1024),
            name="settled_bands",
        )(*outs)
    latest = outs[0]
    full_bands = lax.all_gather(latest, "band", axis=1, tiled=True)
    partial_value = jnp.einsum("nb,nc->bc", full_bands, full_bands, precision=lax.Precision.HIGHEST)
    margin = lax.psum(partial_value, "dom")
    norm_value = jnp.sqrt(jnp.sum(margin * margin) + 1e-06)
    full_width = margin.shape[0]
    offset = lax.axis_index("band") * s.width
    scaled_cols = lax.dynamic_slice_in_dim(margin, offset, s.width, 1) / norm_value
    identity_cols = lax.dynamic_slice_in_dim(
        jnp.eye(full_width, dtype=jnp.float32), offset, s.width, 1
    )
    mixing = (3.0 * identity_cols - scaled_cols) / 2.0
    return jnp.dot(full_bands, mixing, precision=lax.Precision.HIGHEST)


def solution(mesh):
    return jax.shard_map(
        on_device,
        mesh=mesh,
        in_specs=(P("dom", "band"), P("dom", None, None), P("dom", None), P("dom")),
        out_specs=P("dom", "band"),
        check_vma=False,
    )
```

```python
import functools
import types

import jax
import jax.numpy as jnp
from jax import lax
from jax.experimental import pallas as pl
from jax.experimental.pallas import tpu as pltpu
from jax.sharding import PartitionSpec as P

DEGREE = 2


cheb_centre = 1.0
cheb_half = 1.6

f32 = jnp.float32
bf16 = jnp.bfloat16
MESH = pl.DeviceIdType.MESH
VMEM_LIMIT = 58 * 1024 * 1024


def round_up(value, step):
    return (value + step - 1) // step * step


def halves(value):
    high = value.astype(bf16)
    low = (value - high.astype(f32)).astype(bf16)
    return high, low


def dot(left, right):
    return jnp.dot(left, right, preferred_element_type=f32)


def dot_tn(left, right):
    return lax.dot_general(left, right, (((0,), (0,)), ((), ())), preferred_element_type=f32)


def dot_nt(left, right):
    return lax.dot_general(left, right, (((1,), (1,)), ((), ())), preferred_element_type=f32)


class Sizes:
    def __init__(self, n_dom, n_band, own, width, cells, nodes, face):
        self.n_dom, self.n_band = n_dom, n_band
        self.own, self.width = own, width
        self.cells, self.nodes, self.face = cells, nodes, face
        self.own_pad = round_up(own, 128)
        self.face_pad = round_up(face, 128)
        self.rows = round_up(nodes, 16)
        self.lanes = round_up(nodes, 128)
        self.blocks = 2 if width % 256 == 0 else 1
        self.block = width // self.blocks
        self.depth = round_up(own + face, 128)
        self.base = own // 128 * 128
        self.half_pad = round_up(own // 2, 128)
        self.pieces = 2
        self.chips = n_dom // 2
        self.chunk = width // n_dom
        self.gram = (
            n_band == 2
            and n_dom % 2 == 0
            and n_dom > 2
            and width % (8 * n_dom) == 0
            and width % 128 == 0
            and own % 32 == 0
        )


def start_all(copies):
    for copy in copies:
        copy.start()


def wait_all(copies):
    for copy in copies:
        copy.wait()


def filter_steps(s, greet, ready, done, wave_ref, ops_ref, map_ref, face_ref, result_ref, w):
    me = lax.axis_index("dom")
    right = lax.rem(me + 1, s.n_dom)
    left = lax.rem(me + s.n_dom - 1, s.n_dom)
    C, R, L, W = s.cells, s.rows, s.lanes, s.block
    known = s.own + s.face
    blocks = range(s.blocks)

    def span(q):
        return pl.ds(2 * q * W, 2 * W)

    def split_store(ref, first, value, q=0):
        high, low = halves(value)
        ref[pl.ds(first, value.shape[0]), pl.ds(2 * q * W, W)] = high
        ref[pl.ds(first, value.shape[0]), pl.ds((2 * q + 1) * W, W)] = low

    def merged(wide, q=0):
        return wide[:, 2 * q * W : (2 * q + 1) * W] + wide[:, (2 * q + 1) * W : (2 * q + 2) * W]

    inputs = []
    for k, (source, target) in enumerate(zip((map_ref, face_ref, wave_ref, ops_ref), (w.map, w.face, w.wave, w.ops))):
        inputs.append(pltpu.make_async_copy(source, target, w.input_sem.at[k]))
        inputs[k].start()
    greet()
    map_ref, face_ref, wave_ref = w.map, w.face, w.wave
    inputs[0].wait()
    inputs[1].wait()

    w.index[...] = jnp.full(w.index.shape, -1.0, f32)
    w.index[pl.ds(0, C), pl.ds(0, s.nodes)] = map_ref[...].astype(f32)
    w.index[pl.ds(C, 1), pl.ds(0, s.face)] = face_ref[...].astype(f32)
    columns = jnp.transpose(w.index[...])

    def one_hot(match):
        return jnp.where(match, 1.0, 0.0).astype(bf16)

    def iota(shape, axis):
        return lax.broadcasted_iota(jnp.int32, shape, axis).astype(f32)

    faces = columns[: s.face, C : C + 1]
    w.face_rows[...] = one_hot(faces == iota((s.face, s.own_pad), 1))
    w.vec[pl.ds(s.own, s.depth - s.own), :] = jnp.zeros((s.depth - s.own, w.vec.shape[1]), bf16)
    inputs[2].wait()
    for q in blocks:
        split_store(w.vec, 0, wave_ref[:, pl.ds(q * W, W)], q)
    lower = dot(w.face_rows[...], w.vec[pl.ds(0, s.own_pad), :])
    for q in blocks:
        w.face_send[q] = merged(lower, q)

    def remote(send, recv, send_sem, recv_sem, target):
        return pltpu.make_async_remote_copy(
            src_ref=send, dst_ref=recv, send_sem=send_sem, recv_sem=recv_sem,
            device_id={"dom": target}, device_id_type=MESH)

    def face_copy(q):
        return remote(w.face_send.at[q], w.face_recv.at[q], w.face_ssem.at[q], w.face_rsem.at[q], left)

    def back_copy(step, q):
        return remote(w.back_send.at[step, q], w.back_recv.at[step, q],
                      w.back_ssem.at[step, q], w.back_rsem.at[step, q], right)

    def edge_copy(step, q):
        return remote(w.edge_send.at[step, q], w.edge_recv.at[step, q],
                      w.edge_ssem.at[step, q], w.edge_rsem.at[step, q], left)

    def setup_take():
        for c in range(C):
            w.take[pl.ds(c * R, R), :] = one_hot(columns[:R, c : c + 1] == iota((R, s.depth), 1))

    def setup_ops():
        w.op_pad[...] = jnp.zeros(w.op_pad.shape, f32)
        inputs[3].wait()
        for c in range(C):
            w.op_pad[c, pl.ds(0, s.nodes), pl.ds(0, s.nodes)] = w.ops[:, c, :]
            high, low = halves(w.op_pad[c])
            w.op_high[c] = high
            w.op_low[c] = low

    def setup_put():
        for c in range(C):
            row = w.index[c : c + 1, pl.ds(0, L)]
            w.put[pl.ds(0, known), pl.ds(c * L, L)] = one_hot(row == iota((known, L), 0))
            w.put[pl.ds(known, s.face), pl.ds(c * L, L)] = one_hot(row == faces)
            if L > R:
                w.prod[pl.ds(c * L + R, L - R), :] = jnp.zeros((L - R, w.prod.shape[1]), bf16)
                w.cell[c, pl.ds(R, L - R), :] = jnp.zeros((L - R, 2 * W), bf16)
        w.put_back[...] = one_hot(w.index[C : C + 1, pl.ds(0, s.face_pad)] == iota((s.own, s.face_pad), 0))
        for q in range(s.blocks):
            w.far[q] = jnp.zeros(w.far.shape[1:], bf16)
            if s.face_pad > s.face:
                w.back[q, pl.ds(s.face, s.face_pad - s.face), :] = jnp.zeros((s.face_pad - s.face, 2 * W), bf16)

    def gather():
        w.part[...] = dot(w.take[:, pl.ds(0, s.own_pad)], w.vec[pl.ds(0, s.own_pad), :])

    def middle(step, q):
        last = step == DEGREE - 1
        if step == 0:
            face_copy(q).wait()
            split_store(w.far.at[q], s.own - s.base, w.face_recv[q])
        for c in range(C):
            rows = pl.ds(c * R, R)
            if step == 0:
                cell = w.part[rows, span(q)] + dot(w.take[rows, pl.ds(s.base, s.depth - s.base)], w.far[q])
            else:
                cell = dot(w.take[rows, :], w.vec[:, span(q)])
            w.cell[c, pl.ds(0, R), :] = cell.astype(bf16)
        for c in range(C):
            wide = dot(w.op_high[c], w.cell[c])
            value = wide[:, :W] + wide[:, W:] + dot(w.op_low[c], w.cell[c, :, pl.ds(0, W)])
            split_store(w.prod, c * L, value, q)
        count = s.face if last else 2 * s.face
        tail = merged(dot(w.put[pl.ds(s.own, count), :], w.prod[:, span(q)]))
        w.back_send[step, q] = tail[: s.face]
        back_copy(step, q).start()
        if not last:
            w.edge_send[step, q] = tail[s.face :]
            edge_copy(step, q).start()

    def scatter():
        wide = dot(w.put[pl.ds(0, s.own), :], w.prod[...])
        for q in blocks:
            w.applied[q] = merged(wide, q)

    def advance(step, applied, current, earlier):
        if step == 0:
            return (applied - cheb_centre * current) / cheb_half
        return 2.0 * (applied - cheb_centre * current) / cheb_half - earlier

    def finish(step, q):
        back_copy(step, q).wait()
        split_store(w.back.at[q], 0, w.back_recv[step, q])
        applied = w.applied[q] + merged(dot(w.put_back[...], w.back[q]))
        columns = pl.ds(q * W, W)

        def stage(k):
            return wave_ref[:, columns] if k == 0 else w.stages[k - 1, :, columns]

        following = advance(step, applied, stage(step), stage(step - 1) if step else None)
        if step == DEGREE - 1:
            result_ref[:, columns] = following
            done(q)
            return
        w.stages[step, :, columns] = following
        split_store(w.vec, 0, following, q)
        edge_copy(step, q).wait()

        def edge(k):
            return w.face_recv[q] if k == 0 else w.edges[k - 1, q]

        outer = advance(step, w.back_send[step, q] + w.edge_recv[step, q], edge(step), edge(step - 1) if step else None)
        w.edges[step, q] = outer
        split_store(w.vec, s.own, outer, q)

    quarter = me * 4 // s.n_dom

    def begin_where(condition):
        @pl.when(condition)
        def _():
            ready()
            for q in blocks:
                face_copy(q).start()

    setup_take()
    begin_where(quarter >= 2)
    setup_ops()
    begin_where(quarter == 1)
    setup_put()
    begin_where(quarter == 0)
    gather()
    for q in blocks:
        middle(0, q)
    scatter()
    for step in range(1, DEGREE):
        for q in blocks:
            finish(step - 1, q)
            middle(step, q)
        scatter()
    for q in blocks:
        finish(DEGREE - 1, q)


def half_rows(s, which):
    return pl.ds(pl.multiple_of(which * (s.own // 2), 16), s.own // 2)


def remote_band(source, target, w, turn, q):
    return pltpu.make_async_remote_copy(
        src_ref=source, dst_ref=target,
        send_sem=w.band_ssem.at[turn, q], recv_sem=w.band_rsem.at[turn, q],
        device_id={"band": 1 - lax.axis_index("band")}, device_id_type=MESH)


def block_copy(w, q):
    return remote_band(w.block_send.at[q], w.block_recv.at[q], w, 0, q)


def piece_copy(s, band_ref, w, q):
    half = s.own // 2
    size = half // s.pieces
    first = lax.axis_index("band") * half + q * size
    return remote_band(band_ref.at[pl.ds(pl.multiple_of(first, 8), size), :], w.far_band.at[pl.ds(q * size, size), :], w, 1, q)


def gram_steps(s, band_ref, wide_ref, total_ref, w):
    me = lax.axis_index("dom")
    band = lax.axis_index("band")
    other = 1 - band
    chip, core = me // 2, lax.rem(me, 2)
    partner = chip * 2 + (1 - core)
    W, half, n, chunk = s.width, s.own // 2, s.chips, s.chunk

    def core_copy(m):
        return pltpu.make_async_remote_copy(
            src_ref=w.sums.at[m, 1 - core], dst_ref=w.core_recv.at[m],
            send_sem=w.core_ssem.at[m], recv_sem=w.core_rsem.at[m],
            device_id={"dom": partner}, device_id_type=MESH)

    upper = chip * 2 // n

    def farthest(i):
        falling, rising = n - 1 - i, i
        falling = falling - (chip - falling + n) // n
        rising = rising + (rising - chip + n) // n
        return (1 - upper) * falling + upper * rising

    def spread(i, source, target, send_sem, recv_sem):
        chip_to = farthest(i)
        slot = lax.rem(chip_to - chip + n, n) - 1
        return pltpu.make_async_remote_copy(
            src_ref=source(chip_to), dst_ref=target(slot),
            send_sem=send_sem.at[i], recv_sem=recv_sem.at[slot],
            device_id={"dom": chip_to * 2 + core}, device_id_type=MESH)

    def scatter_copies(m):
        return [
            spread(i, lambda t: w.pair.at[m, t], lambda slot: w.scat_recv.at[m, slot], w.scat_ssem.at[m], w.scat_rsem.at[m])
            for i in range(n - 1)
        ]

    def gather_copies(m):
        return [
            spread(i, lambda t: w.full.at[m, core, chip], lambda slot: w.full.at[m, core, chip],
                   w.gath_ssem.at[m], w.gath_rsem.at[m])
            for i in range(n - 1)
        ]

    def swap_copy(m):
        return pltpu.make_async_remote_copy(
            src_ref=w.full.at[m, core], dst_ref=w.full.at[m, core],
            send_sem=w.swap_ssem.at[m], recv_sem=w.swap_rsem.at[m],
            device_id={"dom": partner}, device_id_type=MESH)

    def cross_copy():
        return pltpu.make_async_remote_copy(
            src_ref=w.cross_send, dst_ref=w.cross_recv,
            send_sem=w.cross_ssem, recv_sem=w.cross_rsem,
            device_id={"band": other}, device_id_type=MESH)

    def norm_copy():
        return pltpu.make_async_remote_copy(
            src_ref=w.norm_send, dst_ref=w.norm_recv,
            send_sem=w.norm_ssem, recv_sem=w.norm_rsem,
            device_id={"band": other}, device_id_type=MESH)

    def put_sums(m, value):
        w.sums[m] = value.reshape(2, W // 2, W)

    def pair_up(m):
        core_copy(m).wait()
        total = w.sums[m, core] + w.core_recv[m]
        w.pair[m] = total.reshape(n, chunk, W)

    def own_total(m):
        wait_all(scatter_copies(m))
        total = w.pair[m, chip]
        for j in range(n - 1):
            total = total + w.scat_recv[m, j]
        return total

    owned = band_ref.at[pl.ds(0, s.own), :]
    high, low = halves(owned[...])

    def fill(ref, value):
        count, size = value.shape[0], ref.shape[0]
        ref[pl.ds(0, count), :] = value
        if size > count:
            ref[pl.ds(count, size - count), :] = jnp.zeros((size - count, W), bf16)

    fill(w.near_high, high)
    fill(w.near_low, low)
    turned_high, turned_low = halves(jnp.transpose(band_ref[...]))
    put_sums(0, dot(turned_high, w.near_high[...])
             + dot(turned_high, w.near_low[...])
             + dot(turned_low, w.near_high[...]))
    core_copy(0).start()
    pair_up(0)
    start_all(scatter_copies(0))
    same = own_total(0)
    w.full[0, core, chip] = same
    start_all(gather_copies(0))

    for q in range(s.blocks):
        block_copy(w, q).wait()
    rows = half_rows(s, band)
    far_high, far_low = halves(jnp.concatenate([w.block_recv[q] for q in range(s.blocks)], axis=1))
    w.far_high[rows, :] = far_high
    w.far_low[rows, :] = far_low
    near_high, near_low = w.near_high[rows, :], w.near_low[rows, :]
    first = band == 0

    def pick(a, b):
        return jnp.where(first, a, b)

    fill(w.left_high, pick(far_high, near_high))
    fill(w.left_low, pick(far_low, near_low))
    fill(w.right_high, pick(near_high, far_high))
    fill(w.right_low, pick(near_low, far_low))
    put_sums(1, dot_tn(w.left_high[...], w.right_high[...])
             + dot_tn(w.left_high[...], w.right_low[...])
             + dot_tn(w.left_low[...], w.right_high[...]))
    core_copy(1).start()
    for q in range(s.pieces - 1):
        piece_copy(s, owned, w, q).start()
    pair_up(1)
    start_all(scatter_copies(1))

    wait_all(gather_copies(0))
    swap_copy(0).start()
    cross = own_total(1)
    w.cross_send[...] = cross
    cross_copy().start()
    piece_copy(s, owned, w, s.pieces - 1).start()
    swap_copy(0).wait()
    near_block = w.full[0].reshape(W, W)

    def squares(value):
        return (value * value).reshape(W // 8, 8, W).sum(0)

    near_squares = squares(near_block)
    w.norm_send[...] = near_squares
    norm_copy().start()
    block_high, block_low = halves(near_block)
    w.block_high[0] = block_high
    w.block_low[0] = block_low
    cross_copy().wait()
    cross = pick(cross, w.cross_recv[...]) + pick(w.cross_recv[...], cross)
    w.full[1, core, chip] = cross
    start_all(gather_copies(1))
    near_high, near_low = w.near_high[pl.ds(0, s.own), :], w.near_low[pl.ds(0, s.own), :]
    near_wide = dot(near_high, w.block_high[0]) + dot(near_high, w.block_low[0])
    w.near_prod[...] = near_wide + dot(near_low, w.block_high[0])
    for q in range(s.pieces):
        piece_copy(s, owned, w, q).wait()
    rows = half_rows(s, other)
    high, low = halves(w.far_band[...])
    w.far_high[rows, :] = high
    w.far_low[rows, :] = low
    wait_all(gather_copies(1))
    swap_copy(1).start()
    swap_copy(1).wait()
    norm_copy().wait()
    far_block = w.full[1].reshape(W, W)
    total_ref[...] = near_squares + w.norm_recv[...] + 2.0 * squares(far_block)
    far_block = pick(far_block, jnp.transpose(far_block))
    block_high, block_low = halves(far_block)
    w.block_high[1] = block_high
    w.block_low[1] = block_low
    wide = dot(w.far_high[...], w.block_high[1]) + dot(w.far_high[...], w.block_low[1])
    wide_ref[...] = wide + dot(w.far_low[...], w.block_high[1]) + w.near_prod[...]


def settle_kernel(s, wide_ref, band_ref, total_ref, out_ref, stage, sem):
    norm = jnp.sqrt(jnp.full((1, s.width), jnp.sum(total_ref[...]), f32) + 1e-06)
    scale = 0.5 / norm
    size = s.own // 4
    copies = []
    for k in range(4):
        rows = pl.ds(k * size, size)
        stage[rows, :] = 1.5 * band_ref[rows, :] - wide_ref[rows, :] * scale
        copies.append(pltpu.make_async_copy(stage.at[rows, :], out_ref.at[rows, :], sem.at[k]))
        copies[k].start()
    wait_all(copies)


def kernel(s, names, wave_ref, ops_ref, map_ref, face_ref, *refs):
    outs, scratch = refs[: len(refs) - len(names)], refs[len(refs) - len(names) :]
    w = types.SimpleNamespace(**dict(zip(names, scratch)))
    me = lax.axis_index("dom")
    barrier = pltpu.get_barrier_semaphore()
    greeted = [{"dom": lax.rem(me + 1, s.n_dom)}, {"dom": lax.rem(me + s.n_dom - 1, s.n_dom)}]
    if s.gram:
        chip, core = me // 2, lax.rem(me, 2)
        greeted.append({"dom": chip * 2 + (1 - core)})
        greeted.append({"band": 1 - lax.axis_index("band")})
        for j in range(1, s.chips):
            greeted.append({"dom": lax.rem(chip + j, s.chips) * 2 + core})

    def greet():
        for device in greeted:
            pl.semaphore_signal(barrier, inc=1, device_id=device, device_id_type=MESH)

    def ready():
        pl.semaphore_wait(barrier, len(greeted))

    if s.gram:
        wide_ref, band_ref, total_ref = outs
        if s.own_pad > s.own:
            band_ref[pl.ds(s.own, s.own_pad - s.own), :] = jnp.zeros((s.own_pad - s.own, s.width), f32)
        owned = band_ref.at[pl.ds(0, s.own), :]

        def send(q):
            rows = half_rows(s, 1 - lax.axis_index("band"))
            w.block_send[q] = owned[rows, pl.ds(q * s.block, s.block)]
            block_copy(w, q).start()

        filter_steps(s, greet, ready, send, wave_ref, ops_ref, map_ref, face_ref, owned, w)
        gram_steps(s, band_ref, wide_ref, total_ref, w)
    else:
        filter_steps(s, greet, ready, lambda q: None, wave_ref, ops_ref, map_ref, face_ref, outs[0], w)


def scratch_of(s):
    C, R, L, W, n, chunk = s.cells, s.rows, s.lanes, s.width, s.chips, s.chunk
    V, dma = pltpu.VMEM, pltpu.SemaphoreType.DMA
    scratch = dict(
        index=V((128, max(L, s.face_pad)), f32),
        face_rows=V((s.face, s.own_pad), bf16),
        vec=V((s.depth, 2 * W), bf16),
        take=V((C * R, s.depth), bf16),
        put=V((s.own + 2 * s.face, C * L), bf16),
        put_back=V((s.own, s.face_pad), bf16),
        ops=V((s.nodes, C, s.nodes), f32),
        map=V((C, s.nodes), jnp.int32),
        face=V((1, s.face), jnp.int32),
        wave=V((s.own, W), f32),
        input_sem=dma((4,)),
        op_pad=V((C, R, L), f32),
        op_high=V((C, R, L), bf16),
        op_low=V((C, R, L), bf16),
        part=V((C * R, 2 * W), f32),
        applied=V((s.blocks, s.own, s.block), f32),
        cell=V((C, L, 2 * s.block), bf16),
        prod=V((C * L, 2 * W), bf16),
        far=V((s.blocks, s.depth - s.base, 2 * s.block), bf16),
        back=V((s.blocks, s.face_pad, 2 * s.block), bf16),
        stages=V((DEGREE - 1, s.own, W), f32),
        edges=V((DEGREE - 1, s.blocks, s.face, s.block), f32),
        face_send=V((s.blocks, s.face, s.block), f32),
        face_recv=V((s.blocks, s.face, s.block), f32),
        edge_send=V((DEGREE - 1, s.blocks, s.face, s.block), f32),
        edge_recv=V((DEGREE - 1, s.blocks, s.face, s.block), f32),
        back_send=V((DEGREE, s.blocks, s.face, s.block), f32),
        back_recv=V((DEGREE, s.blocks, s.face, s.block), f32),
        face_ssem=dma((s.blocks,)),
        face_rsem=dma((s.blocks,)),
        edge_ssem=dma((DEGREE - 1, s.blocks)),
        edge_rsem=dma((DEGREE - 1, s.blocks)),
        back_ssem=dma((DEGREE, s.blocks)),
        back_rsem=dma((DEGREE, s.blocks)),
    )
    if s.gram:
        scratch |= dict(
            far_band=V((s.own // 2, W), f32),
            block_send=V((s.blocks, s.own // 2, s.block), f32),
            block_recv=V((s.blocks, s.own // 2, s.block), f32),
            near_high=V((s.own_pad, W), bf16),
            near_low=V((s.own_pad, W), bf16),
            left_high=V((s.half_pad, W), bf16),
            left_low=V((s.half_pad, W), bf16),
            right_high=V((s.half_pad, W), bf16),
            right_low=V((s.half_pad, W), bf16),
            far_high=V((s.own, W), bf16),
            far_low=V((s.own, W), bf16),
            near_prod=V((s.own, W), f32),
            block_high=V((2, W, W), bf16),
            block_low=V((2, W, W), bf16),
            sums=V((2, 2, W // 2, W), f32),
            core_recv=V((2, W // 2, W), f32),
            pair=V((2, n, chunk, W), f32),
            scat_recv=V((2, n - 1, chunk, W), f32),
            full=V((2, 2, n, chunk, W), f32),
            cross_send=V((chunk, W), f32),
            cross_recv=V((chunk, W), f32),
            norm_send=V((8, W), f32),
            norm_recv=V((8, W), f32),
            norm_ssem=dma,
            norm_rsem=dma,
            cross_ssem=dma,
            cross_rsem=dma,
            band_ssem=dma((2, max(s.blocks, s.pieces))),
            band_rsem=dma((2, max(s.blocks, s.pieces))),
            core_ssem=dma((2,)),
            core_rsem=dma((2,)),
            swap_ssem=dma((2,)),
            swap_rsem=dma((2,)),
            scat_ssem=dma((2, n - 1)),
            scat_rsem=dma((2, n - 1)),
            gath_ssem=dma((2, n - 1)),
            gath_rsem=dma((2, n - 1)),
        )
    return scratch


def on_device(wavefun, cell_ops, cell_map, face_list):
    s = Sizes(lax.axis_size("dom"), lax.axis_size("band"), wavefun.shape[0], wavefun.shape[1],
              cell_map.shape[0], cell_map.shape[1], face_list.shape[0])
    scratch = scratch_of(s)
    shapes = [wavefun.shape]
    if s.gram:
        shapes += [(s.own_pad, s.width), (8, s.width)]
    inside = pl.BlockSpec(memory_space=pltpu.VMEM)
    outs = pl.pallas_call(
        functools.partial(kernel, s, list(scratch)),
        out_shape=[pltpu.VMEM(shape, f32) if s.gram else jax.ShapeDtypeStruct(shape, f32) for shape in shapes],
        in_specs=[pl.BlockSpec(memory_space=pl.ANY)] * 4,
        out_specs=[inside] * len(shapes),
        scratch_shapes=list(scratch.values()),
        compiler_params=pltpu.CompilerParams(
            collective_id=0, has_side_effects=True, vmem_limit_bytes=VMEM_LIMIT),
        name="filtered_bands",
    )(wavefun, jnp.swapaxes(cell_ops, 0, 1), cell_map, face_list.reshape(1, -1))
    if s.gram:
        return pl.pallas_call(
            functools.partial(settle_kernel, s),
            out_shape=jax.ShapeDtypeStruct(wavefun.shape, f32),
            in_specs=[inside] * 3,
            out_specs=pl.BlockSpec(memory_space=pl.ANY),
            scratch_shapes=[pltpu.VMEM(wavefun.shape, f32), pltpu.SemaphoreType.DMA((4,))],
            compiler_params=pltpu.CompilerParams(vmem_limit_bytes=8 * 1024 * 1024),
            name="settled_bands",
        )(*outs)
    latest = outs[0]
    full_bands = lax.all_gather(latest, "band", axis=1, tiled=True)
    partial_value = jnp.einsum("nb,nc->bc", full_bands, full_bands, precision=lax.Precision.HIGHEST)
    margin = lax.psum(partial_value, "dom")
    norm_value = jnp.sqrt(jnp.sum(margin * margin) + 1e-06)
    full_width = margin.shape[0]
    offset = lax.axis_index("band") * s.width
    scaled_cols = lax.dynamic_slice_in_dim(margin, offset, s.width, 1) / norm_value
    identity_cols = lax.dynamic_slice_in_dim(
        jnp.eye(full_width, dtype=jnp.float32), offset, s.width, 1
    )
    mixing = (3.0 * identity_cols - scaled_cols) / 2.0
    return jnp.dot(full_bands, mixing, precision=lax.Precision.HIGHEST)


def solution(mesh):
    return jax.shard_map(
        on_device,
        mesh=mesh,
        in_specs=(P("dom", "band"), P("dom", None, None), P("dom", None), P("dom")),
        out_specs=P("dom", "band"),
        check_vma=False,
    )
```
